512 devices in a mesh: gx: 8 (over z), gy: 16 (over y, core), row: 4 (over x).
Axes of the slice: x: 4, y: 8, z: 8, core: 2. Of those that a mesh axis runs over, the one named last changes fastest.
Arguments:
- tokens: bfloat16 [4, 3584, 1664], P('row', 'gx', 'gy'), may hold values from -6 to 6
- segments: int32 [4, 3584], P('row'), may hold values from 0 to 31, never falling along the last dimension, each value on 1 to 2016 neighbouring positions
- gain_attn: float32 [1664], replicated, may hold values from 0.1 to 1.9
- w_query: bfloat16 [1664, 1664], P('gx', 'gy'), as said below
- w_key: bfloat16 [1664, 1664], P('gx', 'gy'), as said below
- w_value: bfloat16 [1664, 1664], P('gx', 'gy'), may hold values from -0.15625 to 0.15625
- w_out: bfloat16 [1664, 1664], P('gy'), may hold values from -0.15625 to 0.15625
- gain_mlp: float32 [1664], replicated, may hold values from 0.1 to 1.9
- w_up: bfloat16 [1664, 8192], P('gx', 'gy'), may hold values from -0.15625 to 0.15625
- w_down: bfloat16 [8192, 1664], P('gy', 'gx'), may hold values from -0.0625 to 0.0625
- w_merge: bfloat16 [4, 1664, 1664], P(None, 'gy', 'gx'), may hold values from -0.078125 to 0.078125
- merge_groups: int32 [4, 896, 4], P('row', 'gx'), may hold values from 0 to 447, as said below
- sources: int32 [4, 896], P('row', 'gx'), may hold values from 0 to 447, as said below
Outputs:
- layer_out: bfloat16 [4, 3584, 1664], P('row', 'gx', 'gy')
- returned: bfloat16 [4, 896, 1664], P('row', 'gx', 'gy')
The draws below stay inside these ranges and needn't reach their ends.
Inputs may be any that keep to these rules, and one draw needn't show every extreme that they name: `segments`: ids never fall along a row group's tokens; each of the 32 ids holds 1 to 2016 tokens, one exactly 2016. `merge_groups`: for every row group and every block of 112 merged rows (one index of gx), the four positions of all its groups name each of 0 to 447 exactly once. `sources`: for every block b of 112 merged rows, the values over all row groups at that block name each of 0 to 447 exactly once. `w_query`: a real matrix whose entries lie within -161.2 and 161.2 over the square root of 1664. `w_key`: a real matrix whose entries lie within -4 and 4 over the square root of 1664.
All inputs are finite; a program needn't handle non-finite values.
Results may differ from the reference program's by a relative error of at most 0.029.
Values may be sent and summed in bfloat16 or wider, within the bound.
A program may use at most 64 MiB of HBM per device.

```python
import math
import jax
import jax.numpy as jnp
import numpy as np
from jax import lax

D = 1664
H = 16
HD = 104
FF = 8192
TOK_DEV = 448
SEQ = 3584
MERGE_DEV = 112
MERGED = 896
SEGS = 32
SEG_MOST = 2016
N_GX = 8
N_ROW = 4


def truncated(sub_key, shape):
    return jax.random.truncated_normal(sub_key, -4.0, 4.0, shape, jnp.float32)


def key_base(key):
    return truncated(jax.random.fold_in(key, 11), (D, D)) * D ** (-0.5)


def draw_w_key(key, part):
    return key_base(key).astype(jnp.bfloat16)


def draw_w_query(key, part):
    fresh = truncated(jax.random.fold_in(key, 13), (D, D)) * D ** (-0.5)
    return (3.0 * fresh).astype(jnp.bfloat16)


def draw_merge_groups(key, part):
    key_list = jax.random.split(key, N_ROW * N_GX)
    shuffled = jax.vmap(lambda sub_key: jax.random.permutation(sub_key, TOK_DEV))(key_list)
    return shuffled.reshape(N_ROW, MERGED, 4).astype(jnp.int32)


def draw_sources(key, part):
    key_list = jax.random.split(key, N_GX)
    shuffled = jax.vmap(lambda sub_key: jax.random.permutation(sub_key, N_ROW * MERGE_DEV))(key_list)
    shuffled = shuffled.reshape(N_GX, N_ROW, MERGE_DEV).transpose(1, 0, 2)
    return shuffled.reshape(N_ROW, MERGED).astype(jnp.int32)


def level_of(key, shape, pieces, least, largest):
    def one(position, shards_of):
        draws = jax.random.uniform(jax.random.fold_in(jax.random.fold_in(key, 6), position), (shards_of,), jnp.float32, least / len(pieces), largest / len(pieces))
        return jnp.repeat(jnp.exp(draws), shape[position] // shards_of).reshape((-1,) + (1,) * (len(shape) - position - 1))

    level = one(*pieces[0])
    for cut in pieces[1:]:
        level = level * one(*cut)
    return level


def split_up(count, total, reach, skew):
    loads = [(1 << 20) // math.isqrt(standing ** skew) + 1 for standing in range(2, count + 1)]
    rest, given = total - reach - (count - 1), [1] * (count - 1)
    while rest > 0:
        free = [i for i in range(count - 1) if given[i] < reach]
        whole, left = sum([loads[i] for i in free]), rest
        for i in free:
            extra = min(reach - given[i], max(1, left * loads[i] // whole), rest)
            given[i] = given[i] + extra
            rest = rest - extra
    return np.array([reach] + given)


def uneven(rng, amount, total, limit, slope):
    if amount == 2:
        one = jax.random.randint(rng, (), max(1, total - limit), min(limit, total - 1) + 1)
        return jnp.stack([one, total - one])
    lengths = jnp.asarray(split_up(amount, total, limit, slope), jnp.int32)
    couples = (amount - 1) // 2
    giver, taker = lengths[1:1 + 2 * couples:2], lengths[2:2 + 2 * couples:2]
    slack = jnp.minimum(giver - 1, limit - taker)
    passed = jax.random.randint(jax.random.fold_in(rng, 1), (couples,), 0, 1 << 20) % (slack + 1)
    lengths = lengths.at[1:1 + 2 * couples:2].set(giver - passed).at[2:2 + 2 * couples:2].set(taker + passed)
    return lengths[jax.random.permutation(jax.random.fold_in(rng, 2), amount)]


def gaussian(own_key, extent, width, most, pieces=(), kind=jnp.bfloat16):
    entries = jax.random.normal(own_key, extent, jnp.float32) * width
    if len(pieces) > 0:
        entries = level_of(own_key, extent, pieces, -0.22, 0.18) * entries
    return jnp.clip(entries, min=-most, max=most).astype(kind)


def setup_inputs(seed: int = 0) -> dict:
    keys = jax.random.split(jax.random.key(seed), 14)
    return {
        "tokens": gaussian(keys[0], (N_ROW, SEQ, D), 1.0, 6.0, ((0, 4), (1, 8), (2, 16))),
        "segments": jax.vmap(lambda own: jnp.searchsorted(jnp.cumsum(uneven(own, SEGS, SEQ, SEG_MOST, 2)), jnp.arange(SEQ), side="right"))(jax.random.split(keys[1], N_ROW)).reshape((N_ROW, SEQ)).astype(jnp.int32),
        "gain_attn": jnp.clip(1.0 + 0.18 * jax.random.normal(keys[2], (D,), jnp.float32), 0.1, 1.9),
        "w_query": draw_w_query(jax.random.fold_in(keys[13], 71), 0),
        "w_key": draw_w_key(jax.random.fold_in(keys[13], 71), 0),
        "w_value": gaussian(keys[5], (D, D), D ** -0.5, 0.15625, ((0, 8), (1, 16))),
        "w_out": gaussian(keys[6], (D, D), D ** -0.5, 0.15625, ((0, 16),)),
        "gain_mlp": jnp.clip(1.0 + 0.18 * jax.random.normal(keys[7], (D,), jnp.float32), 0.1, 1.9),
        "w_up": gaussian(keys[8], (D, FF), D ** -0.5, 0.15625, ((0, 8), (1, 16))),
        "w_down": gaussian(keys[9], (FF, D), FF ** -0.5, 0.0625, ((0, 16), (1, 8))),
        "w_merge": gaussian(keys[10], (4, D, D), (4 * D) ** -0.5, 0.078125, ((1, 16), (2, 8))),
        "merge_groups": draw_merge_groups(jax.random.fold_in(keys[13], 71), 0),
        "sources": draw_sources(jax.random.fold_in(keys[13], 71), 0),
    }


EPS = 1e-06
NEG = -1e+30

def normalize(tok_rows, gain):
    tok_rows = tok_rows.astype(jnp.float32)
    row_mean = lax.optimization_barrier(jnp.mean(tok_rows, axis=-1, keepdims=True))
    centred = tok_rows - row_mean
    row_var = lax.optimization_barrier(jnp.mean(centred * centred, axis=-1, keepdims=True))
    return (centred * lax.rsqrt(row_var + EPS) * gain.astype(jnp.float32)).astype(jnp.bfloat16)

def reference(tokens, segments, gain_attn, w_query, w_key, w_value, w_out, gain_mlp, w_up, w_down, w_merge, merge_groups, sources):
    scale = HD ** (-0.5)

    def by_head(matrix):
        return matrix.reshape(SEQ, H, HD).transpose(1, 0, 2)

    def one_group(inputs):
        tok_rows, seg_ids = inputs
        normed = normalize(tok_rows, gain_attn)
        queries = jnp.dot(normed, w_query, preferred_element_type=jnp.float32).astype(jnp.bfloat16)
        key_rows = jnp.dot(normed, w_key, preferred_element_type=jnp.float32).astype(jnp.bfloat16)
        value_rows = jnp.dot(normed, w_value, preferred_element_type=jnp.float32).astype(jnp.bfloat16)
        same_seg = seg_ids[:, None] == seg_ids[None, :]

        def one_head(parts):
            q_head, k_head, v_head = parts
            scores = jnp.dot(q_head, k_head.T, preferred_element_type=jnp.float32) * scale
            scores = jnp.where(same_seg, scores, NEG)
            row_top = lax.optimization_barrier(jnp.max(scores, axis=-1, keepdims=True))
            weights = jnp.where(same_seg, jnp.exp(scores - row_top), 0.0)
            row_total = lax.optimization_barrier(jnp.sum(weights, axis=-1, keepdims=True))
            mixed = jnp.dot(weights.astype(jnp.bfloat16), v_head, preferred_element_type=jnp.float32)
            return mixed / row_total
        attended = lax.map(one_head, (by_head(queries), by_head(key_rows), by_head(value_rows)))
        attended = attended.transpose(1, 0, 2).reshape(SEQ, D).astype(jnp.bfloat16)
        after_attn = (tok_rows.astype(jnp.float32) + jnp.dot(attended, w_out, preferred_element_type=jnp.float32)).astype(jnp.bfloat16)
        normed_mlp = normalize(after_attn, gain_mlp)
        hidden = jax.nn.gelu(jnp.dot(normed_mlp, w_up, preferred_element_type=jnp.float32), approximate=False).astype(jnp.bfloat16)
        return (after_attn.astype(jnp.float32) + jnp.dot(hidden, w_down, preferred_element_type=jnp.float32)).astype(jnp.bfloat16)
    layer_out = lax.map(one_group, (tokens, segments))
    block_start = jnp.arange(MERGED, dtype=jnp.int32) // MERGE_DEV * TOK_DEV
    merge_matrix = w_merge.reshape(4 * D, D)

    def merge_group(inputs):
        out_rows, group_ids = inputs
        picked = out_rows[(group_ids + block_start[:, None]).astype(jnp.int32)].reshape(MERGED, 4 * D)
        return jnp.dot(picked, merge_matrix, preferred_element_type=jnp.float32).astype(jnp.bfloat16)
    merged = lax.map(merge_group, (layer_out, merge_groups))
    slot_block = jnp.arange(MERGED, dtype=jnp.int32) // MERGE_DEV
    source_group = (sources // MERGE_DEV).astype(jnp.int32)
    source_row = (slot_block[None, :] * MERGE_DEV + sources % MERGE_DEV).astype(jnp.int32)
    returned = merged[source_group, source_row]
    return (layer_out, returned)
```

```python
import functools

import jax
import jax.numpy as jnp
from jax import lax
from jax.experimental import pallas as pl
from jax.experimental.pallas import tpu as pltpu
from jax.sharding import PartitionSpec as P

MESH = pl.DeviceIdType.MESH
F32 = jnp.float32
BF16 = jnp.bfloat16
EPS = 1e-06
NEG = -1e30

TOK = 448
HD = 104
SLOTS = 16
NZ = 8
NY = 8
D = 1664
FF_DEV = 512
GROUPS = 112
SCALE = HD ** (-0.5)

SEM_COUNTS = dict(
    loc=7,
    tok_y=14,
    tok_s=8,
    att_y=14,
    att_s=8,
    aft_y=14,
    aft_s=8,
    kv=14,
    qkv=14,
    wup=14,
    wdn=14,
    wmg=14,
    wo=15,
    rs_s=8,
    rs_y=7,
    mg_s=1,
    mg_y=7,
    row=3,
)


def erf_gelu(v):
    return 0.5 * v * (1.0 + lax.erf(v * (0.5 ** 0.5)))


def kernel(
    tok_h,
    seg_ref,
    ga_ref,
    wq_h,
    wk_h,
    wv_h,
    wo_ref,
    gm_ref,
    wu_h,
    wd_h,
    wm_h,
    mg_ref,
    src_ref,
    lo_ref,
    ret_ref,
    tok,
    xn,
    wqkv,
    qs,
    kv,
    att,
    aft,
    wout_s,
    wout,
    wup,
    wdn,
    wmg,
    hid,
    pp,
    sb,
    ra,
    rb,
    pk,
    mm,
    sm,
    rm,
    stk,
    seg8,
    qseg,
    gsa,
    gsm,
    m_s,
    l_s,
    acc_s,
    *sems,
):
    gx = lax.axis_index("gx")
    gy = lax.axis_index("gy")
    row = lax.axis_index("row")
    core = lax.rem(gy, 2)
    ypos = gy // 2
    d_a = 1 - 2 * core
    d_w = 1 - 2 * lax.rem(row + core, 2)

    names = list(SEM_COUNTS)
    send = {n: sems[2 * i] for i, n in enumerate(names)}
    recv = {n: sems[2 * i + 1] for i, n in enumerate(names)}

    def gy_at(delta):
        return lax.rem(gy + delta + 32, 16)

    def gx_at(delta):
        return lax.rem(gx + delta + 16, 8)

    def row_at(delta):
        return lax.rem(row + delta + 4, 4)

    def y_at(delta):
        return lax.rem(ypos + delta + 16, 8)

    sib = gy + 1 - 2 * core
    pending = []

    def push(name, idx, src, dst, target):
        copy = pltpu.make_async_remote_copy(
            src_ref=src,
            dst_ref=dst,
            send_sem=send[name].at[idx],
            recv_sem=recv[name].at[idx],
            device_id=target,
            device_id_type=MESH,
        )
        copy.start()
        pending.append(copy)

    def arrive(name, idx, ref):
        pltpu.make_async_remote_copy(
            src_ref=ref,
            dst_ref=ref,
            send_sem=send[name].at[idx],
            recv_sem=recv[name].at[idx],
            device_id={"gy": sib},
            device_id_type=MESH,
        ).wait_recv()

    local = []
    for i, (src, dst) in enumerate(
        (
            (tok_h, tok.at[gy]),
            (wq_h, wqkv.at[gx, 0]),
            (wk_h, wqkv.at[gx, 1]),
            (wv_h, wqkv.at[gx, 2]),
            (wu_h, wup.at[gx]),
            (wd_h, wdn.at[gx]),
            (wm_h, wmg.at[gx]),
        )
    ):
        copy = pltpu.make_async_copy(src, dst, send["loc"].at[i])
        copy.start()
        local.append(copy)

    barrier = pltpu.get_barrier_semaphore()
    for d in range(1, 16):
        pl.semaphore_signal(barrier, inc=1, device_id={"gy": gy_at(d)}, device_id_type=MESH)
    for d in (1, -1):
        pl.semaphore_signal(barrier, inc=1, device_id={"gx": gx_at(d)}, device_id_type=MESH)
    for d in (1, 2, 3):
        pl.semaphore_signal(barrier, inc=1, device_id={"row": row_at(d)}, device_id_type=MESH)
    pl.semaphore_wait(barrier, 20)

    half = TOK // 2

    class GatherY:
        def __init__(self, name, buf):
            self.name, self.buf = name, buf

        def part(self, slot, ch):
            return self.buf.at[slot, pl.ds(ch * half, half)]

        def ahead(self, s, ch):
            slot = gy_at(-2 * (s - 1) * d_a)
            ref = self.part(slot, ch)
            push(self.name + "_y", 2 * (s - 1) + ch, ref, ref, {"gy": gy_at(2 * d_a)})

        def back(self, s, ch):
            slot = gy_at(2 * (s - 1) * d_a)
            ref = self.part(slot, ch)
            push(self.name + "_y", 8 + 2 * (s - 1) + ch, ref, ref, {"gy": gy_at(-2 * d_a)})

        def across(self, idx, slot):
            ref = self.buf.at[slot]
            push(self.name + "_s", idx, ref, ref, {"gy": sib})

        def start(self):
            for ch in (0, 1):
                self.ahead(1, ch)
                self.back(1, ch)
            self.across(0, gy)

        def step(self, s):
            slot_a = gy_at(-2 * s * d_a)
            slot_b = gy_at(2 * s * d_a)
            for ch in (0, 1):
                arrive(self.name + "_y", 2 * (s - 1) + ch, self.part(slot_a, ch))
                if s < 4:
                    self.ahead(s + 1, ch)
                if s < 4:
                    arrive(self.name + "_y", 8 + 2 * (s - 1) + ch, self.part(slot_b, ch))
                    if s < 3:
                        self.back(s + 1, ch)
            self.across(s, slot_a)
            if s < 4:
                self.across(4 + s, slot_b)

        def finish(self):
            arrive(self.name + "_s", 0, self.buf.at[sib])
            for s in range(1, 5):
                arrive(self.name + "_s", s, self.buf.at[lax.rem(sib + 2 * s * d_a + 32, 16)])
                if s < 4:
                    arrive(self.name + "_s", 4 + s, self.buf.at[lax.rem(sib - 2 * s * d_a + 32, 16)])

    class Weights:
        def __init__(self, name, buf, parts):
            self.name, self.buf, self.parts = name, buf, parts

        def ref(self, slot, p):
            return self.parts(self.buf, slot, p)

        def ahead(self, s):
            slot = gx_at(-(s - 1) * d_w)
            for p in (0, 1):
                ref = self.ref(slot, p)
                push(self.name, 2 * (s - 1) + p, ref, ref, {"gx": gx_at(d_w)})

        def step(self, s):
            slot = gx_at(-s * d_w)
            for p in (0, 1):
                ref = self.ref(slot, p)
                arrive(self.name, 2 * (s - 1) + p, ref)
                if s < 4:
                    push(self.name, 2 * s + p, ref, ref, {"gx": gx_at(d_w)})
                    side = d_a if p == 0 else -d_a
                    push(self.name, 8 + 2 * (s - 1) + p, ref, ref, {"row": row_at(side)})

        def finish(self):
            for s in (1, 2, 3):
                for p in (0, 1):
                    arrive(self.name, 8 + 2 * (s - 1) + p, self.ref(gx_at(s * d_w), p))

    def cut(at, end):
        def parts(buf, slot, p):
            return buf.at[slot, pl.ds(0, at)] if p == 0 else buf.at[slot, pl.ds(at, end - at)]

        return parts

    g_tok = GatherY("tok", tok)
    g_att = GatherY("att", att)
    g_aft = GatherY("aft", aft)
    w_qkv = Weights("qkv", wqkv, cut(2, 3))
    w_up = Weights("wup", wup, cut(112, 208))
    w_dn = Weights("wdn", wdn, cut(256, 512))
    w_mg = Weights("wmg", wmg, cut(2, 4))

    local[0].wait()
    g_tok.start()
    for i in (1, 2, 3):
        local[i].wait()
    w_qkv.ahead(1)

    for j in range(SLOTS):
        wout_s[j] = wo_ref[:, j * HD : (j + 1) * HD]
        gsa[j] = ga_ref[:, j * HD : (j + 1) * HD]
        gsm[j] = gm_ref[:, j * HD : (j + 1) * HD]
    for j in range(NZ):
        seg8[j : j + 1, :] = seg_ref[:, j * TOK : (j + 1) * TOK]
    own_row = seg8[pl.ds(gx, 1), :]
    eye = lax.broadcasted_iota(jnp.int32, (TOK, TOK), 0) == lax.broadcasted_iota(
        jnp.int32, (TOK, TOK), 1
    )
    qseg[...] = jnp.sum(jnp.where(eye, own_row.astype(F32), 0.0), axis=1, keepdims=True)

    for s in (1, 2, 3, 4):
        g_tok.step(s)
        w_qkv.step(s)
    g_tok.finish()

    def norm(src, gains, out):
        rows = 64

        def chunk(r, carry):
            at = pl.ds(pl.multiple_of(r * rows, rows), rows)
            total = src[0, at, :].astype(F32)
            for j in range(1, SLOTS):
                total += src[j, at, :].astype(F32)
            mean = jnp.sum(total, axis=-1, keepdims=True) * (1.0 / D)
            square = jnp.zeros((rows, HD), F32)
            for j in range(SLOTS):
                gap = src[j, at, :].astype(F32) - mean
                square += gap * gap
            var = jnp.sum(square, axis=-1, keepdims=True) * (1.0 / D)
            rstd = lax.rsqrt(var + EPS)
            for j in range(SLOTS):
                gap = src[j, at, :].astype(F32) - mean
                out[j // 2, at, (j % 2) * HD : (j % 2 + 1) * HD] = (gap * rstd * gains[j]).astype(BF16)
            return carry

        lax.fori_loop(0, TOK // rows, chunk, 0)

    norm(tok, gsa, xn)
    w_qkv.finish()

    rows2 = TOK // 2

    def project(r, carry):
        at = pl.ds(pl.multiple_of(r * rows2, rows2), rows2)
        for m in (1, 2, 0):
            total = jnp.zeros((rows2, HD), F32)
            for j in range(NZ):
                total += jnp.dot(xn[j, at, :], wqkv[j, m], preferred_element_type=F32)
            if m == 0:
                qs[at, :] = total.astype(BF16)
            else:
                kv[gx, m - 1, at, :] = total.astype(BF16)
        return carry

    lax.fori_loop(0, 2, project, 0)

    def kv_ahead(s):
        slot = gx_at(-(s - 1) * d_a)
        for p in (0, 1):
            ref = kv.at[slot, p]
            push("kv", 2 * (s - 1) + p, ref, ref, {"gx": gx_at(d_a)})

    def kv_back(s):
        slot = gx_at((s - 1) * d_a)
        for p in (0, 1):
            ref = kv.at[slot, p]
            push("kv", 8 + 2 * (s - 1) + p, ref, ref, {"gx": gx_at(-d_a)})

    kv_ahead(1)
    kv_back(1)
    local[4].wait()
    w_up.ahead(1)
    for d in range(1, 16):
        to = gy_at(d)
        push("wo", d - 1, wout_s.at[to], wout.at[gy], {"gy": to})
    wout[gy] = wout_s[gy]

    rows4 = TOK // 4

    def attend(block, first):
        key_seg = seg8[pl.ds(block, 1), :].astype(F32)

        def chunk(r, carry):
            at = pl.ds(pl.multiple_of(r * rows4, rows4), rows4)
            scores = (
                lax.dot_general(
                    qs[at, :], kv[block, 0], (((1,), (1,)), ((), ())), preferred_element_type=F32
                )
                * SCALE
            )
            scores = jnp.where(qseg[at, :] == key_seg, scores, NEG)
            top = jnp.max(scores, axis=-1, keepdims=True)
            if not first:
                old_top = m_s[at, :]
                top = jnp.maximum(old_top, top)
            weights = jnp.exp(scores - top)
            total = jnp.sum(weights, axis=-1, keepdims=True)
            mixed = jnp.dot(weights.astype(BF16), kv[block, 1], preferred_element_type=F32)
            if not first:
                fade = jnp.exp(old_top - top)
                total += l_s[at, :] * fade
                mixed += acc_s[at, :] * fade
            m_s[at, :] = top
            l_s[at, :] = total
            acc_s[at, :] = mixed
            return carry

        lax.fori_loop(0, TOK // rows4, chunk, 0)

    attend(gx, True)
    for s in (1, 2, 3, 4):
        slot_a, slot_b = gx_at(-s * d_a), gx_at(s * d_a)
        for p in (0, 1):
            arrive("kv", 2 * (s - 1) + p, kv.at[slot_a, p])
            if s < 4:
                ref = kv.at[slot_a, p]
                push("kv", 2 * s + p, ref, ref, {"gx": gx_at(d_a)})
            if s < 4:
                arrive("kv", 8 + 2 * (s - 1) + p, kv.at[slot_b, p])
                if s < 3:
                    ref = kv.at[slot_b, p]
                    push("kv", 8 + 2 * s + p, ref, ref, {"gx": gx_at(-d_a)})
        attend(slot_a, False)
        if s < 4:
            attend(slot_b, False)
        w_up.step(s)

    att[gy] = (acc_s[...] / l_s[...]).astype(BF16)
    g_att.start()
    local[5].wait()
    w_dn.ahead(1)
    for d in range(1, 16):
        arrive("wo", d - 1, wout.at[gy_at(-d)])
    for s in (1, 2, 3, 4):
        g_att.step(s)
        w_dn.step(s)
    g_att.finish()

    def out_proj(r, carry):
        at = pl.ds(pl.multiple_of(r * rows2, rows2), rows2)
        total = jnp.zeros((rows2, HD), F32)
        for j in range(SLOTS):
            total += jnp.dot(att[j, at, :], wout[j], preferred_element_type=F32)
        aft[gy, at, :] = (tok[gy, at, :].astype(F32) + total).astype(BF16)
        return carry

    lax.fori_loop(0, 2, out_proj, 0)

    g_aft.start()
    local[6].wait()
    w_mg.ahead(1)
    for s in (1, 2, 3, 4):
        g_aft.step(s)
        w_mg.step(s)
    g_aft.finish()
    norm(aft, gsm, xn)
    w_up.finish()

    def mlp_up(r, carry):
        at = pl.ds(pl.multiple_of(r * rows4, rows4), rows4)
        total = jnp.zeros((rows4, FF_DEV), F32)
        for j in range(NZ):
            total += jnp.dot(xn[j, at, :], wup[j], preferred_element_type=F32)
        hid[at, :] = erf_gelu(total).astype(BF16)
        return carry

    lax.fori_loop(0, 4, mlp_up, 0)
    w_dn.finish()

    order = (4, -3, 3, -2, 2, -1, 1, 0)
    for i, d in enumerate(order):
        dest = y_at(d * d_a)
        for h in (0, 1):
            pass

        def mlp_down(r, carry):
            at = pl.ds(pl.multiple_of(r * rows2, rows2), rows2)
            part = jnp.dot(hid[at, :], wdn[dest], preferred_element_type=F32)
            pp[dest, 0, at, :] = part[:, :HD].astype(BF16)
            pp[dest, 1, at, :] = part[:, HD:].astype(BF16)
            return carry

        lax.fori_loop(0, 2, mlp_down, 0)
        push("rs_s", i, pp.at[dest, 1 - core], sb.at[dest], {"gy": sib})

    def fold(dest, extra):
        pp[dest, core] = (pp[dest, core].astype(F32) + extra.astype(F32)).astype(BF16)

    for i, d in enumerate(order):
        arrive("rs_s", i, sb.at[y_at(-d * d_a)])

    def fold_all(j, carry):
        fold(j, sb[j])
        return carry

    lax.fori_loop(0, NY, fold_all, 0)
    ahead, behind = {"gy": gy_at(2 * d_a)}, {"gy": gy_at(-2 * d_a)}
    push("rs_y", 0, pp.at[y_at(4 * d_a), core], ra.at[0], ahead)
    push("rs_y", 4, pp.at[y_at(-3 * d_a), core], rb.at[0], behind)
    for s in (1, 2, 3):
        arrive("rs_y", s - 1, ra.at[s - 1])
        dest = y_at((4 - s) * d_a)
        fold(dest, ra[s - 1])
        push("rs_y", s, pp.at[dest, core], ra.at[s], ahead)
        if s < 3:
            arrive("rs_y", 4 + s - 1, rb.at[s - 1])
            dest = y_at(-(3 - s) * d_a)
            fold(dest, rb[s - 1])
            push("rs_y", 4 + s, pp.at[dest, core], rb.at[s], behind)
    arrive("rs_y", 6, rb.at[2])
    arrive("rs_y", 3, ra.at[3])
    lo_ref[...] = (
        aft[gy].astype(F32)
        + (pp[ypos, core].astype(F32) + ra[3].astype(F32) + rb[2].astype(F32))
    ).astype(BF16)

    w_mg.finish()
    spot = lax.broadcasted_iota(jnp.int32, (GROUPS, TOK), 1)
    for k in range(4):
        pick = jnp.where(mg_ref[:, k : k + 1] == spot, 1.0, 0.0).astype(BF16)
        pk[k] = jnp.dot(pick, lo_ref[...], preferred_element_type=F32).astype(BF16)

    def merge(j, carry):
        total = jnp.zeros((GROUPS, 2 * HD), F32)
        for k in range(4):
            total += jnp.dot(pk[k], wmg[j, k], preferred_element_type=F32)
        mm[0, j] = total[:, :HD].astype(BF16)
        mm[1, j] = total[:, HD:].astype(BF16)
        return carry

    lax.fori_loop(0, NY, merge, 0)
    push("mg_s", 0, mm.at[1 - core], sm, {"gy": sib})
    arrive("mg_s", 0, sm)
    mm[core] = (mm[core].astype(F32) + sm[...].astype(F32)).astype(BF16)
    for d in (4, 3, 5, 2, 6, 1, 7):
        push("mg_y", d - 1, mm.at[core, y_at(d)], rm.at[d - 1], {"gy": gy_at(2 * d)})
    total = mm[core, ypos].astype(F32)
    for d in range(1, 8):
        arrive("mg_y", d - 1, rm.at[d - 1])
    for d in range(1, 8):
        total += rm[d - 1].astype(F32)
    stk[row] = total.astype(BF16)
    for d in (1, 2, 3):
        push("row", d - 1, stk.at[row], stk.at[row], {"row": row_at(d)})
    eye2 = lax.broadcasted_iota(jnp.int32, (GROUPS, GROUPS), 0) == lax.broadcasted_iota(
        jnp.int32, (GROUPS, GROUPS), 1
    )
    wanted = jnp.sum(jnp.where(eye2, src_ref[...].astype(F32), 0.0), axis=1, keepdims=True)
    for d in (1, 2, 3):
        arrive("row", d - 1, stk.at[row_at(-d)])
    place = lax.broadcasted_iota(jnp.int32, (GROUPS, GROUPS), 1).astype(F32)
    total = jnp.zeros((GROUPS, HD), F32)
    for r in range(4):
        pick = jnp.where(wanted == place + float(GROUPS * r), 1.0, 0.0).astype(BF16)
        total += jnp.dot(pick, stk[r], preferred_element_type=F32)
    ret_ref[...] = total.astype(BF16)

    for copy in pending:
        copy.wait_send()


def body(
    tokens,
    segments,
    gain_attn,
    w_query,
    w_key,
    w_value,
    w_out,
    gain_mlp,
    w_up,
    w_down,
    w_merge,
    merge_groups,
    sources,
):
    anyspace = pl.BlockSpec(memory_space=pl.ANY)
    vmem = pl.BlockSpec(memory_space=pltpu.VMEM)
    scratch = [
        pltpu.VMEM((SLOTS, TOK, HD), BF16),
        pltpu.VMEM((NZ, TOK, 2 * HD), BF16),
        pltpu.VMEM((NZ, 3, 2 * HD, HD), BF16),
        pltpu.VMEM((TOK, HD), BF16),
        pltpu.VMEM((NZ, 2, TOK, HD), BF16),
        pltpu.VMEM((SLOTS, TOK, HD), BF16),
        pltpu.VMEM((SLOTS, TOK, HD), BF16),
        pltpu.VMEM((SLOTS, HD, HD), BF16),
        pltpu.VMEM((SLOTS, HD, HD), BF16),
        pltpu.VMEM((NZ, 2 * HD, FF_DEV), BF16),
        pltpu.VMEM((NZ, FF_DEV, 2 * HD), BF16),
        pltpu.VMEM((NZ, 4, HD, 2 * HD), BF16),
        pltpu.VMEM((TOK, FF_DEV), BF16),
        pltpu.VMEM((NY, 2, TOK, HD), BF16),
        pltpu.VMEM((NY, TOK, HD), BF16),
        pltpu.VMEM((4, TOK, HD), BF16),
        pltpu.VMEM((3, TOK, HD), BF16),
        pltpu.VMEM((4, GROUPS, HD), BF16),
        pltpu.VMEM((2, NY, GROUPS, HD), BF16),
        pltpu.VMEM((NY, GROUPS, HD), BF16),
        pltpu.VMEM((7, GROUPS, HD), BF16),
        pltpu.VMEM((4, GROUPS, HD), BF16),
        pltpu.VMEM((NZ, TOK), jnp.int32),
        pltpu.VMEM((TOK, 1), F32),
        pltpu.VMEM((SLOTS, 1, HD), F32),
        pltpu.VMEM((SLOTS, 1, HD), F32),
        pltpu.VMEM((TOK, 1), F32),
        pltpu.VMEM((TOK, 1), F32),
        pltpu.VMEM((TOK, HD), F32),
    ]
    for count in SEM_COUNTS.values():
        scratch += [pltpu.SemaphoreType.DMA((count,)), pltpu.SemaphoreType.DMA((count,))]
    layer_out, returned = pl.pallas_call(
        kernel,
        out_shape=(
            jax.ShapeDtypeStruct((TOK, HD), BF16),
            jax.ShapeDtypeStruct((GROUPS, HD), BF16),
        ),
        in_specs=[
            anyspace,
            vmem,
            vmem,
            anyspace,
            anyspace,
            anyspace,
            vmem,
            vmem,
            anyspace,
            anyspace,
            anyspace,
            vmem,
            vmem,
        ],
        out_specs=(vmem, vmem),
        scratch_shapes=scratch,
        compiler_params=pltpu.CompilerParams(
            collective_id=0, has_side_effects=True, vmem_limit_bytes=48 << 20
        ),
        name="layer",
    )(
        tokens[0],
        segments,
        gain_attn.reshape(1, D),
        w_query,
        w_key,
        w_value,
        w_out,
        gain_mlp.reshape(1, D),
        w_up,
        w_down,
        w_merge,
        merge_groups[0],
        sources,
    )
    return (layer_out[None], returned[None])


def solution(mesh):
    placed = (
        P("row", "gx", "gy"),
        P("row", None),
        P(),
        P("gx", "gy"),
        P("gx", "gy"),
        P("gx", "gy"),
        P("gy", None),
        P(),
        P("gx", "gy"),
        P("gy", "gx"),
        P(None, "gy", "gx"),
        P("row", "gx", None),
        P("row", "gx"),
    )
    return jax.shard_map(
        body,
        mesh=mesh,
        in_specs=placed,
        out_specs=(P("row", "gx", "gy"), P("row", "gx", "gy")),
        check_vma=False,
    )
```

```python
import functools

import jax
import jax.numpy as jnp
from jax import lax
from jax.experimental import pallas as pl
from jax.experimental.pallas import tpu as pltpu
from jax.sharding import PartitionSpec as P

MESH = pl.DeviceIdType.MESH
F32 = jnp.float32
BF16 = jnp.bfloat16
EPS = 1e-06
NEG = -1e30

TOK = 448
HD = 104
SLOTS = 16
NZ = 8
NY = 8
D = 1664
FF_DEV = 512
GROUPS = 112
EXP2 = HD ** (-0.5) * 1.4426950408889634

HALF = TOK // 2

LOCAL = 13
SEM_COUNTS = dict(
    tok_y=14,
    tok_s=8,
    kv=14,
    qkv=14,
    wup=7,
    wdn=7,
    wmg=7,
    bulk=2,
    wo=8,
    swap=2,
    att_y=14,
    aft_y=14,
    rs_y=14,
    mg_s=1,
    mg_y=7,
    row=3,
)


def erf_gelu(v):
    return 0.5 * v * (1.0 + lax.erf(v * (0.5 ** 0.5)))


def kernel(
    tok_h,
    seg_h,
    ga_h,
    wq_h,
    wk_h,
    wv_h,
    wo_h,
    gm_h,
    wu_h,
    wd_h,
    wm_h,
    mg_h,
    src_h,
    lo_ref,
    ret_ref,
    tok,
    xn,
    wqkv,
    qs,
    kv,
    att,
    aft,
    wout_s,
    wout,
    wup,
    wdn,
    wmg,
    hid,
    pp,
    ra,
    rb,
    lo_s,
    swap_s,
    pk,
    mm,
    sm,
    rm,
    stk,
    seg8,
    qseg,
    gsa,
    gsm,
    m_s,
    l_s,
    acc_s,
    tok_t,
    wo_ref,
    seg_ref,
    mg_ref,
    src_ref,
    ga_ref,
    gm_ref,
    loc_sem,
    *sems,
):
    gx = lax.axis_index("gx")
    gy = lax.axis_index("gy")
    row = lax.axis_index("row")
    core = lax.rem(gy, 2)
    ypos = gy // 2
    d_a = 1 - 2 * core
    d_w = 1 - 2 * lax.rem(row + core, 2)

    names = list(SEM_COUNTS)
    send = {n: sems[2 * i] for i, n in enumerate(names)}
    recv = {n: sems[2 * i + 1] for i, n in enumerate(names)}

    def gy_at(delta):
        return lax.rem(gy + delta + 32, 16)

    def gx_at(delta):
        return lax.rem(gx + delta + 16, 8)

    def row_at(delta):
        return lax.rem(row + delta + 4, 4)

    def y_at(delta):
        return lax.rem(ypos + delta + 16, 8)

    sib = gy + 1 - 2 * core
    pending = []

    def push(name, idx, src, dst, target):
        copy = pltpu.make_async_remote_copy(
            src_ref=src,
            dst_ref=dst,
            send_sem=send[name].at[idx],
            recv_sem=recv[name].at[idx],
            device_id=target,
            device_id_type=MESH,
        )
        copy.start()
        pending.append(copy)

    def arrive(name, idx, ref):
        pltpu.make_async_remote_copy(
            src_ref=ref,
            dst_ref=ref,
            send_sem=send[name].at[idx],
            recv_sem=recv[name].at[idx],
            device_id={"gy": sib},
            device_id_type=MESH,
        ).wait_recv()

    local = []
    for i, (src, dst) in enumerate(
        (
            (tok_h, tok_t),
            (wq_h, wqkv.at[gx, 0]),
            (wk_h, wqkv.at[gx, 1]),
            (wv_h, wqkv.at[gx, 2]),
            (wo_h, wo_ref),
            (seg_h, seg_ref),
            (mg_h, mg_ref),
            (src_h, src_ref),
            (ga_h, ga_ref),
            (gm_h, gm_ref),
            (wu_h, wup.at[core, gx]),
            (wd_h, wdn.at[core, gx]),
            (wm_h, wmg.at[gx]),
        )
    ):
        copy = pltpu.make_async_copy(src, dst, loc_sem.at[i])
        copy.start()
        local.append(copy)
    local[0].wait()
    tok[gy] = jnp.transpose(tok_t[...])

    barrier = pltpu.get_barrier_semaphore()
    for d in range(1, 8):
        pl.semaphore_signal(barrier, inc=1, device_id={"gy": gy_at(2 * d)}, device_id_type=MESH)
    pl.semaphore_signal(barrier, inc=1, device_id={"gy": sib}, device_id_type=MESH)
    for d in (1, -1):
        pl.semaphore_signal(barrier, inc=1, device_id={"gx": gx_at(d)}, device_id_type=MESH)
    for d in (1, 2, 3):
        pl.semaphore_signal(barrier, inc=1, device_id={"row": row_at(d)}, device_id_type=MESH)
    pl.semaphore_wait(barrier, 13)

    class Ring:
        def __init__(self, name, part):
            self.name, self.part = name, part

        def ahead(self, s, p):
            ref = self.part(-(s - 1) * d_a, p)
            push(self.name, 2 * (s - 1) + p, ref, ref, {"gy": gy_at(2 * d_a)})

        def back(self, s, p):
            ref = self.part((s - 1) * d_a, p)
            push(self.name, 8 + 2 * (s - 1) + p, ref, ref, {"gy": gy_at(-2 * d_a)})

        def start(self, p):
            self.ahead(1, p)
            self.back(1, p)

        def step(self, s):
            for p in (0, 1):
                arrive(self.name, 2 * (s - 1) + p, self.part(-s * d_a, p))
                if s < 4:
                    self.ahead(s + 1, p)
                    arrive(self.name, 8 + 2 * (s - 1) + p, self.part(s * d_a, p))
                    if s < 3:
                        self.back(s + 1, p)

    def tok_part(k, p):
        return tok.at[gy_at(2 * k), pl.ds(p * HALF, HALF)]

    def across(idx, slot):
        push("tok_s", idx, tok.at[slot], tok.at[slot], {"gy": sib})

    def pair_part(buf):
        def part(k, p):
            slot = 2 * y_at(k) + (core if p == 0 else 1 - core)
            return buf.at[slot]

        return part

    class Weights:
        def __init__(self, name, buf, cuts):
            self.name, self.buf, self.cuts = name, buf, cuts
            self.n = len(cuts)

        def ref(self, slot, p):
            at, size = self.cuts[p]
            return self.buf.at[slot, pl.ds(at, size)]

        def ahead(self):
            for p in range(self.n):
                ref = self.ref(gx, p)
                push(self.name, p, ref, ref, {"gx": gx_at(d_w)})

        def step(self, s):
            slot = gx_at(-s * d_w)
            for p in range(self.n):
                ref = self.ref(slot, p)
                arrive(self.name, self.n * (s - 1) + p, ref)
                if s < 4:
                    push(self.name, self.n * s + p, ref, ref, {"gx": gx_at(d_w)})
                    side = d_a if p % 2 == 0 else -d_a
                    push(self.name, self.n * (s + 3) + p, ref, ref, {"row": row_at(side)})

        def finish(self):
            for s in (1, 2, 3):
                for p in range(self.n):
                    arrive(self.name, self.n * (s + 3) + p, self.ref(gx_at(s * d_w), p))

    g_tok = Ring("tok_y", tok_part)
    g_att = Ring("att_y", pair_part(att))
    g_aft = Ring("aft_y", pair_part(aft))
    w_qkv = Weights("qkv", wqkv, ((0, 2), (2, 1)))
    w_up = Weights("wup", wup.at[core], ((0, 208),))
    w_dn = Weights("wdn", wdn.at[core], ((0, 208),))
    w_mg = Weights("wmg", wmg, ((0, 4),))

    g_tok.start(0)
    g_tok.start(1)
    across(0, gy)
    for i in (1, 2, 3):
        local[i].wait()
    w_qkv.ahead()
    for i in range(4, 10):
        local[i].wait()

    for j in range(SLOTS):
        gsa[j] = ga_ref[:, j * HD : (j + 1) * HD]
        gsm[j] = gm_ref[:, j * HD : (j + 1) * HD]
    for j in range(NY):
        wout_s[j] = wo_ref[:, j * 2 * HD : (j + 1) * 2 * HD]
    for j in range(NZ):
        seg8[j : j + 1, :] = seg_ref[:, j * TOK : (j + 1) * TOK]
    own_row = seg8[pl.ds(gx, 1), :]
    eye = lax.broadcasted_iota(jnp.int32, (TOK, TOK), 0) == lax.broadcasted_iota(
        jnp.int32, (TOK, TOK), 1
    )
    qseg[...] = jnp.sum(jnp.where(eye, own_row.astype(F32), 0.0), axis=1, keepdims=True)

    for s in (1, 2, 3, 4):
        g_tok.step(s)
        across(s, gy_at(-2 * s * d_a))
        if s < 4:
            across(4 + s, gy_at(2 * s * d_a))
        w_qkv.step(s)
    local[10].wait()
    w_up.ahead()
    arrive("tok_s", 0, tok.at[sib])
    for s in (1, 2, 3, 4):
        arrive("tok_s", s, tok.at[lax.rem(sib + 2 * s * d_a + 32, 16)])
        if s < 4:
            arrive("tok_s", 4 + s, tok.at[lax.rem(sib - 2 * s * d_a + 32, 16)])

    def norm(src, gains, out, count, rows):

        def chunk(r, carry):
            at = pl.ds(pl.multiple_of(r * rows, rows), rows)
            total = src[0, at, :].astype(F32)
            for j in range(1, SLOTS):
                total += src[j, at, :].astype(F32)
            mean = jnp.sum(total, axis=-1, keepdims=True) * (1.0 / D)
            square = jnp.zeros((rows, HD), F32)
            for j in range(SLOTS):
                gap = src[j, at, :].astype(F32) - mean
                square += gap * gap
            var = jnp.sum(square, axis=-1, keepdims=True) * (1.0 / D)
            rstd = lax.rsqrt(var + EPS)
            for j in range(SLOTS):
                gap = src[j, at, :].astype(F32) - mean
                out[j // 2, at, (j % 2) * HD : (j % 2 + 1) * HD] = (gap * rstd * gains[j]).astype(BF16)
            return carry

        lax.fori_loop(0, count // rows, chunk, 0)

    norm(tok, gsa, xn, TOK, 64)
    w_qkv.finish()

    rows2 = TOK // 2

    def project(m):
        def chunk(r, carry):
            at = pl.ds(pl.multiple_of(r * rows2, rows2), rows2)
            total = jnp.zeros((rows2, HD), F32)
            for j in range(NZ):
                total += jnp.dot(xn[j, at, :], wqkv[j, m], preferred_element_type=F32)
            if m == 0:
                qs[at, :] = total.astype(BF16)
            else:
                kv[gx, m - 1, at, :] = total.astype(BF16)
            return carry

        lax.fori_loop(0, 2, chunk, 0, unroll=True)

    def kv_ahead(s, p):
        ref = kv.at[gx_at(-(s - 1) * d_a), p]
        push("kv", 2 * (s - 1) + p, ref, ref, {"gx": gx_at(d_a)})

    def kv_back(s, p):
        ref = kv.at[gx_at((s - 1) * d_a), p]
        push("kv", 8 + 2 * (s - 1) + p, ref, ref, {"gx": gx_at(-d_a)})

    for p in (0, 1):
        project(p + 1)
        kv_ahead(1, p)
        kv_back(1, p)
    project(0)
    for d in range(1, 8):
        to = y_at(d)
        push("wo", d - 1, wout_s.at[to], wout.at[core, ypos], {"gy": gy_at(2 * d)})
    wout[core, ypos] = wout_s[ypos]

    rows4 = TOK // 4

    def attend(block, first=False, part=None):
        start = 0 if part is None else part * HALF
        key_seg = seg8[pl.ds(block, 1), :].astype(F32)

        def chunk(r, carry):
            at = pl.ds(pl.multiple_of(start + r * rows4, 16), rows4)
            scores = lax.dot_general(
                qs[at, :], kv[block, 0], (((1,), (1,)), ((), ())), preferred_element_type=F32
            )
            scores = jnp.where(qseg[at, :] == key_seg, scores, NEG)
            top = jnp.max(scores, axis=-1, keepdims=True)
            if not first:
                old_top = m_s[at, :]
                top = jnp.maximum(old_top, top)
            weights = jnp.exp2((scores - top) * EXP2)
            total = jnp.sum(weights, axis=-1, keepdims=True)
            mixed = jnp.dot(weights.astype(BF16), kv[block, 1], preferred_element_type=F32)
            if not first:
                fade = jnp.exp2((old_top - top) * EXP2)
                total += l_s[at, :] * fade
                mixed += acc_s[at, :] * fade
            m_s[at, :] = top
            l_s[at, :] = total
            acc_s[at, :] = mixed
            return carry

        lax.fori_loop(0, (TOK if part is None else HALF) // rows4, chunk, 0, unroll=True)

    attend(gx, True)
    w_up.step(1)
    for s in (1, 2, 3, 4):
        for p in (0, 1):
            arrive("kv", 2 * (s - 1) + p, kv.at[gx_at(-s * d_a), p])
            if s < 4:
                kv_ahead(s + 1, p)
                arrive("kv", 8 + 2 * (s - 1) + p, kv.at[gx_at(s * d_a), p])
                if s < 3:
                    kv_back(s + 1, p)
            if s > 1:
                attend(gx_at((-1 if p == 0 else 1) * (s - 1) * d_a))
        if s > 1:
            w_up.step(s)
        if s == 2:
            local[11].wait()
            w_dn.ahead()
        if s == 4:
            w_dn.step(1)

    theirs, mine = pl.multiple_of((1 - core) * HALF, HALF), pl.multiple_of(core * HALF, HALF)

    def attended(start):
        at = pl.ds(start, HALF)
        return (acc_s[at, :] / l_s[at, :]).astype(BF16)

    last = gx_at(-4 * d_a)
    attend(last, part=1 - core)
    swap_s[0] = attended(theirs)
    push("swap", 0, swap_s.at[0], att.at[gy], {"gy": sib})
    attend(last, part=core)
    att[gy] = attended(mine)
    g_att.start(0)
    for d in range(1, 8):
        arrive("wo", d - 1, wout.at[core, y_at(-d)])
    push("wo", 7, wout.at[core], wout.at[core], {"gy": sib})
    arrive("swap", 0, att.at[sib])
    g_att.start(1)
    w_up.finish()
    push("bulk", 0, wup.at[core], wup.at[core], {"gy": sib})
    local[12].wait()
    w_mg.ahead()
    for s in (1, 2, 3, 4):
        g_att.step(s)
        if s == 1:
            w_dn.step(2)
        if s == 2:
            w_mg.step(1)
        if s == 3:
            w_dn.step(3)
    arrive("wo", 7, wout.at[1 - core])

    total = jnp.zeros((HALF, 2 * HD), F32)
    for j in range(SLOTS):
        total += jnp.dot(att[j], wout[j % 2, j // 2], preferred_element_type=F32)
    for h in (0, 1):
        own = tok[2 * ypos + h, pl.ds(mine, HALF), :].astype(F32)
        aft[2 * ypos + h] = (own + total[:, h * HD : (h + 1) * HD]).astype(BF16)

    g_aft.start(0)
    g_aft.start(1)
    w_mg.step(2)
    for s in (1, 2, 3, 4):
        g_aft.step(s)
        if s == 1:
            w_dn.step(4)
        if s == 2:
            w_mg.step(3)
        if s == 3:
            w_dn.finish()
            push("bulk", 1, wdn.at[core], wdn.at[core], {"gy": sib})
    norm(aft, gsm, xn, HALF, 32)
    arrive("bulk", 0, wup.at[1 - core])

    def mlp_up(r, carry):
        g = r // 2
        at = pl.ds(pl.multiple_of((r % 2) * rows4, rows4), rows4)
        total = jnp.zeros((rows4, FF_DEV), F32)
        for j in range(NZ):
            total += jnp.dot(xn[j, at, :], wup[g, j], preferred_element_type=F32)
        hid[g, at, :] = erf_gelu(total).astype(BF16)
        return carry

    lax.fori_loop(0, 4, mlp_up, 0)
    w_mg.step(4)
    arrive("bulk", 1, wdn.at[1 - core])

    def mlp_down(d):
        dest = y_at(d * d_a)
        part = jnp.zeros((HALF, 2 * HD), F32)
        for g in (0, 1):
            part += lax.dot_general(
                hid[g], wdn[g, dest], (((1,), (1,)), ((), ())), preferred_element_type=F32
            )
        pp[dest, 0] = part[:, :HD].astype(BF16)
        pp[dest, 1] = part[:, HD:].astype(BF16)

    def fold(dest, h, extra):
        pp[dest, h] = (pp[dest, h].astype(F32) + extra.astype(F32)).astype(BF16)

    ahead, behind = {"gy": gy_at(2 * d_a)}, {"gy": gy_at(-2 * d_a)}
    far, near = y_at(4 * d_a), y_at(-3 * d_a)
    mlp_down(4)
    for h in (0, 1):
        push("rs_y", h, pp.at[far, h], ra.at[0, h], ahead)
    mlp_down(-3)
    for h in (0, 1):
        push("rs_y", 8 + h, pp.at[near, h], rb.at[0, h], behind)
    for d in (3, -2, 2, -1, 1, 0):
        mlp_down(d)
    for s in (1, 2, 3):
        to_a, to_b = y_at((4 - s) * d_a), y_at(-(3 - s) * d_a)
        for h in (0, 1):
            arrive("rs_y", 2 * (s - 1) + h, ra.at[s - 1, h])
            fold(to_a, h, ra[s - 1, h])
            push("rs_y", 2 * s + h, pp.at[to_a, h], ra.at[s, h], ahead)
            if s < 3:
                arrive("rs_y", 8 + 2 * (s - 1) + h, rb.at[s - 1, h])
                fold(to_b, h, rb[s - 1, h])
                push("rs_y", 8 + 2 * s + h, pp.at[to_b, h], rb.at[s, h], behind)
    for h in (0, 1):
        arrive("rs_y", 12 + h, rb.at[2, h])
        arrive("rs_y", 6 + h, ra.at[3, h])

    def layer_rows(h):
        mlp_sum = pp[ypos, h].astype(F32) + ra[3, h].astype(F32) + rb[2, h].astype(F32)
        return (aft[2 * ypos + h].astype(F32) + mlp_sum).astype(BF16)

    swap_s[1] = layer_rows(1 - core)
    push("swap", 1, swap_s.at[1], lo_s.at[pl.ds(mine, HALF)], {"gy": sib})
    lo_s[pl.ds(mine, HALF), :] = layer_rows(core)
    w_mg.finish()
    arrive("swap", 1, lo_s.at[pl.ds(theirs, HALF)])
    lo_ref[...] = jnp.transpose(lo_s[...])

    spot = lax.broadcasted_iota(jnp.int32, (GROUPS, TOK), 1).astype(F32)
    eye2 = lax.broadcasted_iota(jnp.int32, (GROUPS, GROUPS), 0) == lax.broadcasted_iota(
        jnp.int32, (GROUPS, GROUPS), 1
    )
    for k in range(4):
        member = jnp.sum(
            jnp.where(eye2, mg_ref[k : k + 1, :].astype(F32), 0.0), axis=1, keepdims=True
        )
        pick = jnp.where(member == spot, 1.0, 0.0).astype(BF16)
        pk[k] = jnp.dot(pick, lo_s[...], preferred_element_type=F32).astype(BF16)

    def merge(j, carry):
        total = jnp.zeros((GROUPS, 2 * HD), F32)
        for k in range(4):
            total += jnp.dot(pk[k], wmg[j, k], preferred_element_type=F32)
        mm[0, j] = total[:, :HD].astype(BF16)
        mm[1, j] = total[:, HD:].astype(BF16)
        return carry

    lax.fori_loop(0, NY, merge, 0)
    push("mg_s", 0, mm.at[1 - core], sm, {"gy": sib})
    arrive("mg_s", 0, sm)
    mm[core] = (mm[core].astype(F32) + sm[...].astype(F32)).astype(BF16)
    for d in (4, 3, 5, 2, 6, 1, 7):
        push("mg_y", d - 1, mm.at[core, y_at(d)], rm.at[d - 1], {"gy": gy_at(2 * d)})
    total = mm[core, ypos].astype(F32)
    for d in range(1, 8):
        arrive("mg_y", d - 1, rm.at[d - 1])
    for d in range(1, 8):
        total += rm[d - 1].astype(F32)
    stk[row] = total.astype(BF16)
    for d in (1, 2, 3):
        push("row", d - 1, stk.at[row], stk.at[row], {"row": row_at(d)})
    wanted = jnp.sum(jnp.where(eye2, src_ref[...].astype(F32), 0.0), axis=1, keepdims=True)
    for d in (1, 2, 3):
        arrive("row", d - 1, stk.at[row_at(-d)])
    place = lax.broadcasted_iota(jnp.int32, (GROUPS, GROUPS), 1).astype(F32)
    total = jnp.zeros((GROUPS, HD), F32)
    for r in range(4):
        pick = jnp.where(wanted == place + float(GROUPS * r), 1.0, 0.0).astype(BF16)
        total += jnp.dot(pick, stk[r], preferred_element_type=F32)
    ret_ref[...] = jnp.transpose(total.astype(BF16))

    for copy in pending:
        copy.wait_send()


def body(
    tokens,
    segments,
    gain_attn,
    w_query,
    w_key,
    w_value,
    w_out,
    gain_mlp,
    w_up,
    w_down,
    w_merge,
    merge_groups,
    sources,
):
    anyspace = pl.BlockSpec(memory_space=pl.ANY)
    vmem = pl.BlockSpec(memory_space=pltpu.VMEM)
    scratch = [
        pltpu.VMEM((SLOTS, TOK, HD), BF16),
        pltpu.VMEM((NZ, TOK, 2 * HD), BF16),
        pltpu.VMEM((NZ, 3, 2 * HD, HD), BF16),
        pltpu.VMEM((TOK, HD), BF16),
        pltpu.VMEM((NZ, 2, TOK, HD), BF16),
        pltpu.VMEM((SLOTS, HALF, HD), BF16),
        pltpu.VMEM((SLOTS, HALF, HD), BF16),
        pltpu.VMEM((NY, HD, 2 * HD), BF16),
        pltpu.VMEM((2, NY, HD, 2 * HD), BF16),
        pltpu.VMEM((2, NZ, 2 * HD, FF_DEV), BF16),
        pltpu.VMEM((2, NZ, 2 * HD, FF_DEV), BF16),
        pltpu.VMEM((NZ, 4, HD, 2 * HD), BF16),
        pltpu.VMEM((2, HALF, FF_DEV), BF16),
        pltpu.VMEM((NY, 2, HALF, HD), BF16),
        pltpu.VMEM((4, 2, HALF, HD), BF16),
        pltpu.VMEM((3, 2, HALF, HD), BF16),
        pltpu.VMEM((TOK, HD), BF16),
        pltpu.VMEM((2, HALF, HD), BF16),
        pltpu.VMEM((4, GROUPS, HD), BF16),
        pltpu.VMEM((2, NY, GROUPS, HD), BF16),
        pltpu.VMEM((NY, GROUPS, HD), BF16),
        pltpu.VMEM((7, GROUPS, HD), BF16),
        pltpu.VMEM((4, GROUPS, HD), BF16),
        pltpu.VMEM((NZ, TOK), jnp.int32),
        pltpu.VMEM((TOK, 1), F32),
        pltpu.VMEM((SLOTS, 1, HD), F32),
        pltpu.VMEM((SLOTS, 1, HD), F32),
        pltpu.VMEM((TOK, 1), F32),
        pltpu.VMEM((TOK, 1), F32),
        pltpu.VMEM((TOK, HD), F32),
        pltpu.VMEM((HD, TOK), BF16),
        pltpu.VMEM((HD, D), BF16),
        pltpu.VMEM((1, NZ * TOK), jnp.int32),
        pltpu.VMEM((4, GROUPS), jnp.int32),
        pltpu.VMEM((1, GROUPS), jnp.int32),
        pltpu.VMEM((1, D), F32),
        pltpu.VMEM((1, D), F32),
        pltpu.SemaphoreType.DMA((LOCAL,)),
    ]
    for count in SEM_COUNTS.values():
        scratch += [pltpu.SemaphoreType.DMA((count,)), pltpu.SemaphoreType.DMA((count,))]
    layer_out, returned = pl.pallas_call(
        kernel,
        out_shape=(
            jax.ShapeDtypeStruct((HD, TOK), BF16),
            jax.ShapeDtypeStruct((HD, GROUPS), BF16),
        ),
        in_specs=[anyspace] * 13,
        out_specs=(vmem, vmem),
        scratch_shapes=scratch,
        compiler_params=pltpu.CompilerParams(
            collective_id=0, has_side_effects=True, vmem_limit_bytes=60 << 20
        ),
        name="layer",
    )(
        tokens[0].T,
        segments,
        gain_attn.reshape(1, D),
        w_query,
        w_key,
        w_value,
        w_out,
        gain_mlp.reshape(1, D),
        w_up,
        w_down.T,
        w_merge,
        merge_groups[0].T,
        sources,
    )
    return (layer_out.T[None], returned.T[None])


def solution(mesh):
    placed = (
        P("row", "gx", "gy"),
        P("row", None),
        P(),
        P("gx", "gy"),
        P("gx", "gy"),
        P("gx", "gy"),
        P("gy", None),
        P(),
        P("gx", "gy"),
        P("gy", "gx"),
        P(None, "gy", "gx"),
        P("row", "gx", None),
        P("row", "gx"),
    )
    return jax.shard_map(
        body,
        mesh=mesh,
        in_specs=placed,
        out_specs=(P("row", "gx", "gy"), P("row", "gx", "gy")),
        check_vma=False,
    )
```

```python
import functools

import jax
import jax.numpy as jnp
from jax import lax
from jax.experimental import pallas as pl
from jax.experimental.pallas import tpu as pltpu
from jax.sharding import PartitionSpec as P

MESH = pl.DeviceIdType.MESH
F32 = jnp.float32
BF16 = jnp.bfloat16
EPS = 1e-06
NEG = -1e30

TOK = 448
HD = 104
SLOTS = 16
NZ = 8
NY = 8
D = 1664
FF_DEV = 512
GROUPS = 112
EXP2 = HD ** (-0.5) * 1.4426950408889634

HALF = TOK // 2
PIECE = HALF // 2

LOCAL = 12
SEM_COUNTS = dict(
    tok_y=14,
    tok_s=16,
    kv=14,
    qkv=14,
    wup=7,
    wupx=3,
    wdn=7,
    wmg=7,
    bulk=2,
    wo=8,
    swap=3,
    att_y=14,
    aft_y=14,
    rs_y=14,
    mg_s=8,
    mg_y=7,
    row=3,
)


def erf_gelu(v):
    return 0.5 * v * (1.0 + lax.erf(v * (0.5 ** 0.5)))


def kernel(
    tok_h,
    seg_h,
    gain_h,
    wq_h,
    wk_h,
    wv_h,
    wo_h,
    wu_h,
    wd_h,
    wm_h,
    mg_h,
    src_h,
    lo_ref,
    ret_ref,
    tok,
    xn,
    wqkv,
    qs,
    kv,
    att,
    aft,
    wout_s,
    wout,
    wup,
    wdn,
    wmg,
    hid,
    pp,
    ra,
    rb,
    lo_s,
    swap_s,
    pk,
    mm,
    sm,
    rm,
    stk,
    seg8,
    qseg,
    gsa,
    gsm,
    m_s,
    l_s,
    acc_s,
    tok_t,
    wo_ref,
    seg_ref,
    mg_ref,
    src_ref,
    gain_ref,
    loc_sem,
    *sems,
):
    gx = lax.axis_index("gx")
    gy = lax.axis_index("gy")
    row = lax.axis_index("row")
    core = lax.rem(gy, 2)
    ypos = gy // 2
    d_a = 1 - 2 * core
    d_w = 1 - 2 * lax.rem(row + core, 2)

    names = list(SEM_COUNTS)
    send = {n: sems[2 * i] for i, n in enumerate(names)}
    recv = {n: sems[2 * i + 1] for i, n in enumerate(names)}

    def gy_at(delta):
        return lax.rem(gy + delta + 32, 16)

    def gx_at(delta):
        return lax.rem(gx + delta + 16, 8)

    def row_at(delta):
        return lax.rem(row + delta + 4, 4)

    def y_at(delta):
        return lax.rem(ypos + delta + 16, 8)

    sib = gy + 1 - 2 * core
    pending = []

    def push(name, idx, src, dst, target):
        copy = pltpu.make_async_remote_copy(
            src_ref=src,
            dst_ref=dst,
            send_sem=send[name].at[idx],
            recv_sem=recv[name].at[idx],
            device_id=target,
            device_id_type=MESH,
        )
        copy.start()
        pending.append(copy)

    def arrive(name, idx, ref):
        pltpu.make_async_remote_copy(
            src_ref=ref,
            dst_ref=ref,
            send_sem=send[name].at[idx],
            recv_sem=recv[name].at[idx],
            device_id={"gy": sib},
            device_id_type=MESH,
        ).wait_recv()

    def quarter(r):
        return pl.ds(pl.multiple_of(r * (FF_DEV // 4), FF_DEV // 4), FF_DEV // 4)

    def quarter_ref(slot):
        return wup.at[core, slot, :, quarter(row)]

    local = []
    for i, (src, dst) in enumerate(
        (
            (tok_h, tok_t),
            (wq_h, wqkv.at[gx, 0]),
            (wk_h, wqkv.at[gx, 1]),
            (wv_h, wqkv.at[gx, 2]),
            (wo_h, wo_ref),
            (seg_h, seg_ref),
            (mg_h, mg_ref),
            (src_h, src_ref),
            (gain_h, gain_ref),
            (wu_h.at[:, quarter(row)], quarter_ref(gx)),
            (wd_h, wdn.at[core, gx]),
            (wm_h, wmg.at[gx]),
        )
    ):
        copy = pltpu.make_async_copy(src, dst, loc_sem.at[i])
        copy.start()
        local.append(copy)
    local[0].wait()
    tok[gy] = jnp.transpose(tok_t[...])

    barrier = pltpu.get_barrier_semaphore()
    for d in range(1, 8):
        pl.semaphore_signal(barrier, inc=1, device_id={"gy": gy_at(2 * d)}, device_id_type=MESH)
    pl.semaphore_signal(barrier, inc=1, device_id={"gy": sib}, device_id_type=MESH)
    for d in (1, -1):
        pl.semaphore_signal(barrier, inc=1, device_id={"gx": gx_at(d)}, device_id_type=MESH)
    for d in (1, 2, 3):
        pl.semaphore_signal(barrier, inc=1, device_id={"row": row_at(d)}, device_id_type=MESH)
    pl.semaphore_wait(barrier, 13)

    class Ring:
        def __init__(self, name, part):
            self.name, self.part = name, part

        def ahead(self, s, p):
            ref = self.part(-(s - 1) * d_a, p)
            push(self.name, 2 * (s - 1) + p, ref, ref, {"gy": gy_at(2 * d_a)})

        def back(self, s, p):
            ref = self.part((s - 1) * d_a, p)
            push(self.name, 8 + 2 * (s - 1) + p, ref, ref, {"gy": gy_at(-2 * d_a)})

        def start(self, p):
            self.ahead(1, p)
            self.back(1, p)

        def piece(self, s, p):
            arrive(self.name, 2 * (s - 1) + p, self.part(-s * d_a, p))
            if s < 4:
                self.ahead(s + 1, p)
                arrive(self.name, 8 + 2 * (s - 1) + p, self.part(s * d_a, p))
                if s < 3:
                    self.back(s + 1, p)

        def step(self, s):
            self.piece(s, 0)
            self.piece(s, 1)

    def tok_part(k, p):
        return tok.at[gy_at(2 * k), pl.ds(p * HALF, HALF)]

    def across(idx, k, p):
        ref = tok_part(k, p)
        push("tok_s", 2 * idx + p, ref, ref, {"gy": sib})

    def aft_part(k, p):
        return aft.at[pl.ds(2 * y_at(k), 2), pl.ds(p * PIECE, PIECE)]

    def pair_part(buf):
        def part(k, p):
            slot = 2 * y_at(k) + (core if p == 0 else 1 - core)
            return buf.at[slot]

        return part

    class Weights:
        def __init__(self, name, buf, cuts):
            self.name, self.buf, self.cuts = name, buf, cuts
            self.n = len(cuts)

        def ref(self, slot, p):
            at, size = self.cuts[p]
            return self.buf.at[slot, pl.ds(at, size)]

        def ahead(self):
            for p in range(self.n):
                ref = self.ref(gx, p)
                push(self.name, p, ref, ref, {"gx": gx_at(d_w)})

        def step(self, s):
            slot = gx_at(-s * d_w)
            for p in range(self.n):
                ref = self.ref(slot, p)
                arrive(self.name, self.n * (s - 1) + p, ref)
                if s < 4:
                    push(self.name, self.n * s + p, ref, ref, {"gx": gx_at(d_w)})
                    side = d_a if p % 2 == 0 else -d_a
                    push(self.name, self.n * (s + 3) + p, ref, ref, {"row": row_at(side)})

        def finish(self):
            for s in (1, 2, 3):
                for p in range(self.n):
                    arrive(self.name, self.n * (s + 3) + p, self.ref(gx_at(s * d_w), p))

    g_tok = Ring("tok_y", tok_part)
    g_att = Ring("att_y", pair_part(att))
    g_aft = Ring("aft_y", aft_part)
    w_qkv = Weights("qkv", wqkv, ((0, 2), (2, 1)))

    class Quarters:
        def ahead(self, s):
            ref = quarter_ref(gx_at(-(s - 1) * d_a))
            push("wup", s - 1, ref, ref, {"gx": gx_at(d_a)})

        def back(self, s):
            ref = quarter_ref(gx_at((s - 1) * d_a))
            push("wup", 3 + s, ref, ref, {"gx": gx_at(-d_a)})

        def start(self):
            self.ahead(1)
            self.back(1)

        def step(self, s):
            arrive("wup", s - 1, quarter_ref(gx_at(-s * d_a)))
            if s < 4:
                self.ahead(s + 1)
                arrive("wup", 3 + s, quarter_ref(gx_at(s * d_a)))
                if s < 3:
                    self.back(s + 1)
            else:
                ref = wup.at[core, :, :, quarter(row)]
                for d in (1, 3, 2):
                    push("wupx", d - 1, ref, ref, {"row": row_at(d)})

        def finish(self):
            for d in (1, 2, 3):
                arrive("wupx", d - 1, wup.at[core, :, :, quarter(row_at(-d))])

    w_up = Quarters()
    w_dn = Weights("wdn", wdn.at[core], ((0, 208),))
    w_mg = Weights("wmg", wmg, ((0, 4),))

    g_tok.start(0)
    g_tok.start(1)
    across(0, 0, 0)
    across(0, 0, 1)
    for i in (1, 2, 3):
        local[i].wait()
    w_qkv.ahead()
    for i in range(4, 9):
        local[i].wait()

    for j in range(SLOTS):
        gsa[j] = gain_ref[0:1, j * HD : (j + 1) * HD]
        gsm[j] = gain_ref[1:2, j * HD : (j + 1) * HD]
    for j in range(NY):
        wout_s[j] = wo_ref[:, j * 2 * HD : (j + 1) * 2 * HD]
    for j in range(NZ):
        seg8[j : j + 1, :] = seg_ref[:, j * TOK : (j + 1) * TOK]
    own_row = seg8[pl.ds(gx, 1), :]
    eye = lax.broadcasted_iota(jnp.int32, (TOK, TOK), 0) == lax.broadcasted_iota(
        jnp.int32, (TOK, TOK), 1
    )
    qseg[...] = jnp.sum(jnp.where(eye, own_row.astype(F32), 0.0), axis=1, keepdims=True)

    for s in (1, 2, 3, 4):
        for p in (0, 1):
            g_tok.piece(s, p)
            across(s, -s * d_a, p)
            if s < 4:
                across(4 + s, s * d_a, p)
        w_qkv.step(s)
        if s == 2:
            local[9].wait()
            w_up.start()

    def norm(src, gains, out, start, count, rows):

        def chunk(r, carry):
            at = pl.ds(pl.multiple_of(start + r * rows, 16), rows)
            total = src[0, at, :].astype(F32)
            for j in range(1, SLOTS):
                total += src[j, at, :].astype(F32)
            mean = jnp.sum(total, axis=-1, keepdims=True) * (1.0 / D)
            square = jnp.zeros((rows, HD), F32)
            for j in range(SLOTS):
                gap = src[j, at, :].astype(F32) - mean
                square += gap * gap
            var = jnp.sum(square, axis=-1, keepdims=True) * (1.0 / D)
            rstd = lax.rsqrt(var + EPS)
            for j in range(SLOTS):
                gap = src[j, at, :].astype(F32) - mean
                out[j // 2, at, (j % 2) * HD : (j % 2 + 1) * HD] = (gap * rstd * gains[j]).astype(BF16)
            return carry

        lax.fori_loop(0, count // rows, chunk, 0)

    w_up.step(1)

    def token_slot(slot, p):
        return tok.at[slot, pl.ds(p * HALF, HALF)]

    for p in (0, 1):
        arrive("tok_s", p, token_slot(sib, p))
        for s in (1, 2, 3, 4):
            arrive("tok_s", 2 * s + p, token_slot(lax.rem(sib + 2 * s * d_a + 32, 16), p))
            if s < 4:
                arrive("tok_s", 2 * (4 + s) + p, token_slot(lax.rem(sib - 2 * s * d_a + 32, 16), p))
        norm(tok, gsa, xn, p * HALF, HALF, PIECE)
    w_up.step(2)
    w_qkv.finish()

    rows2 = TOK // 2

    def project(m):
        def chunk(r, carry):
            at = pl.ds(pl.multiple_of(r * rows2, rows2), rows2)
            total = jnp.zeros((rows2, HD), F32)
            for j in range(NZ):
                total += jnp.dot(xn[j, at, :], wqkv[j, m], preferred_element_type=F32)
            if m == 0:
                qs[at, :] = total.astype(BF16)
            else:
                kv[gx, m - 1, at, :] = total.astype(BF16)
            return carry

        lax.fori_loop(0, 2, chunk, 0, unroll=True)

    def kv_ahead(s, p):
        ref = kv.at[gx_at(-(s - 1) * d_a), p]
        push("kv", 2 * (s - 1) + p, ref, ref, {"gx": gx_at(d_a)})

    def kv_back(s, p):
        ref = kv.at[gx_at((s - 1) * d_a), p]
        push("kv", 8 + 2 * (s - 1) + p, ref, ref, {"gx": gx_at(-d_a)})

    for p in (0, 1):
        project(p + 1)
        kv_ahead(1, p)
        kv_back(1, p)
    project(0)
    for d in range(1, 8):
        to = y_at(d)
        push("wo", d - 1, wout_s.at[to], wout.at[core, ypos], {"gy": gy_at(2 * d)})
    wout[core, ypos] = wout_s[ypos]

    rows4 = TOK // 4

    def attend(block, first=False, part=None):
        start = 0 if part is None else part * HALF
        key_seg = seg8[pl.ds(block, 1), :].astype(F32)

        def chunk(r, carry):
            at = pl.ds(pl.multiple_of(start + r * rows4, 16), rows4)
            scores = lax.dot_general(
                qs[at, :], kv[block, 0], (((1,), (1,)), ((), ())), preferred_element_type=F32
            )
            scores = jnp.where(qseg[at, :] == key_seg, scores, NEG)
            top = jnp.max(scores, axis=-1, keepdims=True)
            if not first:
                old_top = m_s[at, :]
                top = jnp.maximum(old_top, top)
            weights = jnp.exp2((scores - top) * EXP2)
            total = jnp.sum(weights, axis=-1, keepdims=True)
            mixed = jnp.dot(weights.astype(BF16), kv[block, 1], preferred_element_type=F32)
            if not first:
                fade = jnp.exp2((old_top - top) * EXP2)
                total += l_s[at, :] * fade
                mixed += acc_s[at, :] * fade
            m_s[at, :] = top
            l_s[at, :] = total
            acc_s[at, :] = mixed
            return carry

        lax.fori_loop(0, (TOK if part is None else HALF) // rows4, chunk, 0, unroll=True)

    attend(gx, True)
    w_up.step(3)
    for s in (1, 2, 3, 4):
        for p in (0, 1):
            arrive("kv", 2 * (s - 1) + p, kv.at[gx_at(-s * d_a), p])
            if s < 4:
                kv_ahead(s + 1, p)
                arrive("kv", 8 + 2 * (s - 1) + p, kv.at[gx_at(s * d_a), p])
                if s < 3:
                    kv_back(s + 1, p)
            if s > 1:
                attend(gx_at((-1 if p == 0 else 1) * (s - 1) * d_a))
        if s == 1:
            w_up.step(4)
        if s == 3:
            local[10].wait()
            w_dn.ahead()

    theirs, mine = pl.multiple_of((1 - core) * HALF, HALF), pl.multiple_of(core * HALF, HALF)

    def attended(start):
        at = pl.ds(start, HALF)
        return (acc_s[at, :] / l_s[at, :]).astype(BF16)

    last = gx_at(-4 * d_a)
    attend(last, part=1 - core)
    swap_s[0] = attended(theirs)
    push("swap", 0, swap_s.at[0], att.at[gy], {"gy": sib})
    attend(last, part=core)
    att[gy] = attended(mine)
    g_att.start(0)
    for d in range(1, 8):
        arrive("wo", d - 1, wout.at[core, y_at(-d)])
    push("wo", 7, wout.at[core], wout.at[core], {"gy": sib})
    arrive("swap", 0, att.at[sib])
    g_att.start(1)
    w_dn.step(1)
    for s in (1, 2, 3, 4):
        g_att.step(s)
        if s == 2:
            w_dn.step(2)
        if s == 3:
            local[11].wait()
            w_mg.ahead()
    arrive("wo", 7, wout.at[1 - core])
    w_up.finish()
    push("bulk", 0, wup.at[core], wup.at[core], {"gy": sib})

    for p in (0, 1):
        at = pl.ds(p * PIECE, PIECE)
        total = jnp.zeros((PIECE, 2 * HD), F32)
        for j in range(SLOTS):
            total += jnp.dot(att[j, at, :], wout[j % 2, j // 2], preferred_element_type=F32)
        for h in (0, 1):
            own = tok[2 * ypos + h, pl.ds(pl.multiple_of(mine + p * PIECE, 16), PIECE), :].astype(F32)
            aft[2 * ypos + h, at, :] = (own + total[:, h * HD : (h + 1) * HD]).astype(BF16)
        g_aft.start(p)
    w_dn.step(3)
    for s in (1, 2, 3):
        g_aft.step(s)
        if s == 1:
            w_mg.step(1)
        if s == 2:
            w_dn.step(4)
        if s == 3:
            w_mg.step(2)
            w_dn.finish()
            push("bulk", 1, wdn.at[core], wdn.at[core], {"gy": sib})
    arrive("bulk", 0, wup.at[1 - core])

    def mlp_up(p):
        at = pl.ds(p * PIECE, PIECE)

        def units(g, carry):
            total = jnp.zeros((PIECE, FF_DEV), F32)
            for j in range(NZ):
                total += jnp.dot(xn[j, at, :], wup[g, j], preferred_element_type=F32)
            hid[g, at, :] = erf_gelu(total).astype(BF16)
            return carry

        lax.fori_loop(0, 2, units, 0)

    def mlp_down(d, p):
        dest = y_at(d * d_a)
        part = jnp.zeros((PIECE, 2 * HD), F32)
        for g in (0, 1):
            part += lax.dot_general(
                hid[g, pl.ds(p * PIECE, PIECE), :],
                wdn[g, dest],
                (((1,), (1,)), ((), ())),
                preferred_element_type=F32,
            )
        pp[dest, p, 0] = part[:, :HD].astype(BF16)
        pp[dest, p, 1] = part[:, HD:].astype(BF16)

    def fold(dest, p, extra):
        pp[dest, p] = (pp[dest, p].astype(F32) + extra.astype(F32)).astype(BF16)

    ahead, behind = {"gy": gy_at(2 * d_a)}, {"gy": gy_at(-2 * d_a)}
    far, near = y_at(4 * d_a), y_at(-3 * d_a)
    for p in (0, 1):
        g_aft.piece(4, p)
        norm(aft, gsm, xn, p * PIECE, PIECE, PIECE)
        mlp_up(p)
        if p == 0:
            arrive("bulk", 1, wdn.at[1 - core])
        mlp_down(4, p)
        push("rs_y", p, pp.at[far, p], ra.at[0, p], ahead)
        mlp_down(-3, p)
        push("rs_y", 8 + p, pp.at[near, p], rb.at[0, p], behind)
    w_mg.step(3)
    for d in (3, -2, 2, -1, 1, 0):
        for p in (0, 1):
            mlp_down(d, p)
    for s in (1, 2, 3):
        to_a, to_b = y_at((4 - s) * d_a), y_at(-(3 - s) * d_a)
        for p in (0, 1):
            arrive("rs_y", 2 * (s - 1) + p, ra.at[s - 1, p])
            fold(to_a, p, ra[s - 1, p])
            push("rs_y", 2 * s + p, pp.at[to_a, p], ra.at[s, p], ahead)
            if s < 3:
                arrive("rs_y", 8 + 2 * (s - 1) + p, rb.at[s - 1, p])
                fold(to_b, p, rb[s - 1, p])
                push("rs_y", 8 + 2 * s + p, pp.at[to_b, p], rb.at[s, p], behind)
        if s == 1:
            w_mg.step(4)

    def layer_rows(p, h):
        mlp_sum = pp[ypos, p, h].astype(F32) + ra[3, p, h].astype(F32) + rb[2, p, h].astype(F32)
        return (aft[2 * ypos + h, pl.ds(p * PIECE, PIECE), :].astype(F32) + mlp_sum).astype(BF16)

    def rows_at(start, p):
        return pl.ds(pl.multiple_of(start + p * PIECE, 16), PIECE)

    for p in (0, 1):
        arrive("rs_y", 12 + p, rb.at[2, p])
        arrive("rs_y", 6 + p, ra.at[3, p])
        swap_s[1, pl.ds(p * PIECE, PIECE), :] = layer_rows(p, 1 - core)
        push("swap", 1 + p, swap_s.at[1, pl.ds(p * PIECE, PIECE)], lo_s.at[rows_at(mine, p)], {"gy": sib})
        lo_s[rows_at(mine, p), :] = layer_rows(p, core)
    w_mg.finish()
    for p in (0, 1):
        arrive("swap", 1 + p, lo_s.at[rows_at(theirs, p)])

    spot = lax.broadcasted_iota(jnp.int32, (GROUPS, TOK), 1).astype(F32)
    eye2 = lax.broadcasted_iota(jnp.int32, (GROUPS, GROUPS), 0) == lax.broadcasted_iota(
        jnp.int32, (GROUPS, GROUPS), 1
    )
    for k in range(4):
        member = jnp.sum(
            jnp.where(eye2, mg_ref[k : k + 1, :].astype(F32), 0.0), axis=1, keepdims=True
        )
        pick = jnp.where(member == spot, 1.0, 0.0).astype(BF16)
        pk[k] = jnp.dot(pick, lo_s[...], preferred_element_type=F32).astype(BF16)

    others = (4, 3, 5, 2, 6, 1, 7, 0)
    for i, d in enumerate(others):
        dest = y_at(d)
        total = jnp.zeros((GROUPS, 2 * HD), F32)
        for k in range(4):
            total += jnp.dot(pk[k], wmg[dest, k], preferred_element_type=F32)
        mm[0, dest] = total[:, :HD].astype(BF16)
        mm[1, dest] = total[:, HD:].astype(BF16)
        push("mg_s", i, mm.at[1 - core, dest], sm.at[dest], {"gy": sib})
    for i, d in enumerate(others):
        dest = y_at(d)
        arrive("mg_s", i, sm.at[dest])
        mm[core, dest] = (mm[core, dest].astype(F32) + sm[dest].astype(F32)).astype(BF16)
        if d:
            push("mg_y", d - 1, mm.at[core, dest], rm.at[d - 1], {"gy": gy_at(2 * d)})
    lo_ref[...] = jnp.transpose(lo_s[...])
    total = mm[core, ypos].astype(F32)
    for d in range(1, 8):
        arrive("mg_y", d - 1, rm.at[d - 1])
    for d in range(1, 8):
        total += rm[d - 1].astype(F32)
    stk[row] = total.astype(BF16)
    for d in (1, 2, 3):
        push("row", d - 1, stk.at[row], stk.at[row], {"row": row_at(d)})
    wanted = jnp.sum(jnp.where(eye2, src_ref[...].astype(F32), 0.0), axis=1, keepdims=True)
    for d in (1, 2, 3):
        arrive("row", d - 1, stk.at[row_at(-d)])
    place = lax.broadcasted_iota(jnp.int32, (GROUPS, GROUPS), 1).astype(F32)
    total = jnp.zeros((GROUPS, HD), F32)
    for r in range(4):
        pick = jnp.where(wanted == place + float(GROUPS * r), 1.0, 0.0).astype(BF16)
        total += jnp.dot(pick, stk[r], preferred_element_type=F32)
    ret_ref[...] = jnp.transpose(total.astype(BF16))

    for copy in pending:
        copy.wait_send()


def body(
    tokens,
    segments,
    gain_attn,
    w_query,
    w_key,
    w_value,
    w_out,
    gain_mlp,
    w_up,
    w_down,
    w_merge,
    merge_groups,
    sources,
):
    anyspace = pl.BlockSpec(memory_space=pl.ANY)
    vmem = pl.BlockSpec(memory_space=pltpu.VMEM)
    scratch = [
        pltpu.VMEM((SLOTS, TOK, HD), BF16),
        pltpu.VMEM((NZ, TOK, 2 * HD), BF16),
        pltpu.VMEM((NZ, 3, 2 * HD, HD), BF16),
        pltpu.VMEM((TOK, HD), BF16),
        pltpu.VMEM((NZ, 2, TOK, HD), BF16),
        pltpu.VMEM((SLOTS, HALF, HD), BF16),
        pltpu.VMEM((SLOTS, HALF, HD), BF16),
        pltpu.VMEM((NY, HD, 2 * HD), BF16),
        pltpu.VMEM((2, NY, HD, 2 * HD), BF16),
        pltpu.VMEM((2, NZ, 2 * HD, FF_DEV), BF16),
        pltpu.VMEM((2, NZ, 2 * HD, FF_DEV), BF16),
        pltpu.VMEM((NZ, 4, HD, 2 * HD), BF16),
        pltpu.VMEM((2, HALF, FF_DEV), BF16),
        pltpu.VMEM((NY, 2, 2, PIECE, HD), BF16),
        pltpu.VMEM((4, 2, 2, PIECE, HD), BF16),
        pltpu.VMEM((3, 2, 2, PIECE, HD), BF16),
        pltpu.VMEM((TOK, HD), BF16),
        pltpu.VMEM((2, HALF, HD), BF16),
        pltpu.VMEM((4, GROUPS, HD), BF16),
        pltpu.VMEM((2, NY, GROUPS, HD), BF16),
        pltpu.VMEM((NY, GROUPS, HD), BF16),
        pltpu.VMEM((7, GROUPS, HD), BF16),
        pltpu.VMEM((4, GROUPS, HD), BF16),
        pltpu.VMEM((NZ, TOK), jnp.int32),
        pltpu.VMEM((TOK, 1), F32),
        pltpu.VMEM((SLOTS, 1, HD), F32),
        pltpu.VMEM((SLOTS, 1, HD), F32),
        pltpu.VMEM((TOK, 1), F32),
        pltpu.VMEM((TOK, 1), F32),
        pltpu.VMEM((TOK, HD), F32),
        pltpu.VMEM((HD, TOK), BF16),
        pltpu.VMEM((HD, D), BF16),
        pltpu.VMEM((1, NZ * TOK), jnp.int32),
        pltpu.VMEM((4, GROUPS), jnp.int32),
        pltpu.VMEM((1, GROUPS), jnp.int32),
        pltpu.VMEM((2, D), F32),
        pltpu.SemaphoreType.DMA((LOCAL,)),
    ]
    for count in SEM_COUNTS.values():
        scratch += [pltpu.SemaphoreType.DMA((count,)), pltpu.SemaphoreType.DMA((count,))]
    layer_out, returned = pl.pallas_call(
        kernel,
        out_shape=(
            jax.ShapeDtypeStruct((HD, TOK), BF16),
            jax.ShapeDtypeStruct((HD, GROUPS), BF16),
        ),
        in_specs=[anyspace] * 12,
        out_specs=(vmem, vmem),
        scratch_shapes=scratch,
        compiler_params=pltpu.CompilerParams(
            collective_id=0, has_side_effects=True, vmem_limit_bytes=60 << 20
        ),
        name="layer",
    )(
        tokens[0].T,
        segments,
        jnp.stack([gain_attn, gain_mlp]),
        w_query,
        w_key,
        w_value,
        w_out,
        w_up,
        w_down.T,
        w_merge,
        merge_groups[0].T,
        sources,
    )
    return (layer_out.T[None], returned.T[None])


def solution(mesh):
    placed = (
        P("row", "gx", "gy"),
        P("row", None),
        P(),
        P("gx", "gy"),
        P("gx", "gy"),
        P("gx", "gy"),
        P("gy", None),
        P(),
        P("gx", "gy"),
        P("gy", "gx"),
        P(None, "gy", "gx"),
        P("row", "gx", None),
        P("row", "gx"),
    )
    return jax.shard_map(
        body,
        mesh=mesh,
        in_specs=placed,
        out_specs=(P("row", "gx", "gy"), P("row", "gx", "gy")),
        check_vma=False,
    )
```

```python
import functools

import jax
import jax.numpy as jnp
from jax import lax
from jax.experimental import pallas as pl
from jax.experimental.pallas import tpu as pltpu
from jax.sharding import PartitionSpec as P

MESH = pl.DeviceIdType.MESH
F32 = jnp.float32
BF16 = jnp.bfloat16
EPS = 1e-06
NEG = -1e30

TOK = 448
HD = 104
SLOTS = 16
NZ = 8
NY = 8
D = 1664
FF_DEV = 512
GROUPS = 112
EXP2 = HD ** (-0.5) * 1.4426950408889634

HALF = TOK // 2
PIECE = HALF // 2

LOCAL = 12
SEM_COUNTS = dict(
    tok_y=14,
    tok_s=16,
    kv=14,
    qkv=14,
    wup=7,
    wupx=3,
    wdn=7,
    wmg=7,
    bulk=2,
    wo=8,
    swap=3,
    att_y=14,
    aft_y=14,
    rs_y=14,
    mg_s=8,
    mg_y=7,
    row=3,
)


def erf_gelu(v):
    return 0.5 * v * (1.0 + lax.erf(v * (0.5 ** 0.5)))


def kernel(
    tok_h,
    seg_h,
    gain_h,
    wq_h,
    wk_h,
    wv_h,
    wo_h,
    wu_h,
    wd_h,
    wm_h,
    mg_h,
    src_h,
    lo_ref,
    ret_ref,
    tok,
    xn,
    wqkv,
    qs,
    kv,
    att,
    aft,
    wout_s,
    wout,
    wup,
    wdn,
    wmg,
    hid,
    pp,
    ra,
    rb,
    lo_s,
    swap_s,
    pk,
    mm,
    sm,
    rm,
    stk,
    seg8,
    qseg,
    gsa,
    gsm,
    m_s,
    l_s,
    acc_s,
    tok_t,
    wo_ref,
    seg_ref,
    mg_ref,
    src_ref,
    gain_ref,
    loc_sem,
    *sems,
):
    gx = lax.axis_index("gx")
    gy = lax.axis_index("gy")
    row = lax.axis_index("row")
    core = lax.rem(gy, 2)
    ypos = gy // 2
    d_a = 1 - 2 * core
    d_w = 1 - 2 * lax.rem(row + core, 2)

    names = list(SEM_COUNTS)
    send = {n: sems[2 * i] for i, n in enumerate(names)}
    recv = {n: sems[2 * i + 1] for i, n in enumerate(names)}

    def gy_at(delta):
        return lax.rem(gy + delta + 32, 16)

    def gx_at(delta):
        return lax.rem(gx + delta + 16, 8)

    def row_at(delta):
        return lax.rem(row + delta + 4, 4)

    def y_at(delta):
        return lax.rem(ypos + delta + 16, 8)

    sib = gy + 1 - 2 * core
    pending = []

    def push(name, idx, src, dst, target):
        copy = pltpu.make_async_remote_copy(
            src_ref=src,
            dst_ref=dst,
            send_sem=send[name].at[idx],
            recv_sem=recv[name].at[idx],
            device_id=target,
            device_id_type=MESH,
        )
        copy.start()
        pending.append(copy)

    def arrive(name, idx, ref):
        pltpu.make_async_remote_copy(
            src_ref=ref,
            dst_ref=ref,
            send_sem=send[name].at[idx],
            recv_sem=recv[name].at[idx],
            device_id={"gy": sib},
            device_id_type=MESH,
        ).wait_recv()

    def quarter(r):
        return pl.ds(pl.multiple_of(r * (FF_DEV // 4), FF_DEV // 4), FF_DEV // 4)

    def quarter_ref(slot):
        return wup.at[core, slot, :, quarter(row)]

    local = []
    for i, (src, dst) in enumerate(
        (
            (tok_h, tok_t),
            (wq_h, wqkv.at[gx, 0]),
            (wk_h, wqkv.at[gx, 1]),
            (wv_h, wqkv.at[gx, 2]),
            (wo_h, wo_ref),
            (seg_h, seg_ref),
            (mg_h, mg_ref),
            (src_h, src_ref),
            (gain_h, gain_ref),
            (wu_h.at[:, quarter(row)], quarter_ref(gx)),
            (wd_h, wdn.at[core, gx]),
            (wm_h, wmg.at[gx]),
        )
    ):
        copy = pltpu.make_async_copy(src, dst, loc_sem.at[i])
        copy.start()
        local.append(copy)
    local[0].wait()
    tok[gy] = jnp.transpose(tok_t[...])

    barrier = pltpu.get_barrier_semaphore()
    for d in range(1, 8):
        pl.semaphore_signal(barrier, inc=1, device_id={"gy": gy_at(2 * d)}, device_id_type=MESH)
    pl.semaphore_signal(barrier, inc=1, device_id={"gy": sib}, device_id_type=MESH)
    for d in (1, -1):
        pl.semaphore_signal(barrier, inc=1, device_id={"gx": gx_at(d)}, device_id_type=MESH)
    for d in (1, 2, 3):
        pl.semaphore_signal(barrier, inc=1, device_id={"row": row_at(d)}, device_id_type=MESH)
    pl.semaphore_wait(barrier, 13)

    class Ring:
        def __init__(self, name, part):
            self.name, self.part = name, part

        def ahead(self, s, p):
            ref = self.part(-(s - 1) * d_a, p)
            push(self.name, 2 * (s - 1) + p, ref, ref, {"gy": gy_at(2 * d_a)})

        def back(self, s, p):
            ref = self.part((s - 1) * d_a, p)
            push(self.name, 8 + 2 * (s - 1) + p, ref, ref, {"gy": gy_at(-2 * d_a)})

        def start(self, p):
            self.ahead(1, p)
            self.back(1, p)

        def piece(self, s, p):
            arrive(self.name, 2 * (s - 1) + p, self.part(-s * d_a, p))
            if s < 4:
                self.ahead(s + 1, p)
                arrive(self.name, 8 + 2 * (s - 1) + p, self.part(s * d_a, p))
                if s < 3:
                    self.back(s + 1, p)

        def step(self, s):
            for p in (0, 1):
                arrive(self.name, 2 * (s - 1) + p, self.part(-s * d_a, p))
                if s < 4:
                    self.ahead(s + 1, p)
            for p in (0, 1):
                if s < 4:
                    arrive(self.name, 8 + 2 * (s - 1) + p, self.part(s * d_a, p))
                    if s < 3:
                        self.back(s + 1, p)

    def tok_part(k, p):
        return tok.at[gy_at(2 * k), pl.ds(p * HALF, HALF)]

    def across(idx, k, p):
        ref = tok_part(k, p)
        push("tok_s", 2 * idx + p, ref, ref, {"gy": sib})

    def aft_part(k, p):
        return aft.at[pl.ds(2 * y_at(k), 2), pl.ds(p * PIECE, PIECE)]

    def pair_part(buf):
        def part(k, p):
            slot = 2 * y_at(k) + (core if p == 0 else 1 - core)
            return buf.at[slot]

        return part

    class Weights:
        def __init__(self, name, buf, cuts):
            self.name, self.buf, self.cuts = name, buf, cuts
            self.n = len(cuts)

        def ref(self, slot, p):
            at, size = self.cuts[p]
            return self.buf.at[slot, pl.ds(at, size)]

        def ahead(self):
            for p in range(self.n):
                ref = self.ref(gx, p)
                push(self.name, p, ref, ref, {"gx": gx_at(d_w)})

        def step(self, s):
            slot = gx_at(-s * d_w)
            for p in range(self.n):
                ref = self.ref(slot, p)
                arrive(self.name, self.n * (s - 1) + p, ref)
                if s < 4:
                    push(self.name, self.n * s + p, ref, ref, {"gx": gx_at(d_w)})
                    side = d_a if p % 2 == 0 else -d_a
                    push(self.name, self.n * (s + 3) + p, ref, ref, {"row": row_at(side)})

        def finish(self):
            for s in (1, 2, 3):
                for p in range(self.n):
                    arrive(self.name, self.n * (s + 3) + p, self.ref(gx_at(s * d_w), p))

    g_tok = Ring("tok_y", tok_part)
    g_att = Ring("att_y", pair_part(att))
    g_aft = Ring("aft_y", aft_part)
    w_qkv = Weights("qkv", wqkv, ((0, 2), (2, 1)))

    class Quarters:
        def ahead(self, s):
            ref = quarter_ref(gx_at(-(s - 1) * d_a))
            push("wup", s - 1, ref, ref, {"gx": gx_at(d_a)})

        def back(self, s):
            ref = quarter_ref(gx_at((s - 1) * d_a))
            push("wup", 3 + s, ref, ref, {"gx": gx_at(-d_a)})

        def start(self):
            self.ahead(1)
            self.back(1)

        def step(self, s):
            arrive("wup", s - 1, quarter_ref(gx_at(-s * d_a)))
            if s < 4:
                self.ahead(s + 1)
                arrive("wup", 3 + s, quarter_ref(gx_at(s * d_a)))
                if s < 3:
                    self.back(s + 1)
            else:
                ref = wup.at[core, :, :, quarter(row)]
                for d in (1, 3, 2):
                    push("wupx", d - 1, ref, ref, {"row": row_at(d)})

        def finish(self):
            for d in (1, 2, 3):
                arrive("wupx", d - 1, wup.at[core, :, :, quarter(row_at(-d))])

    w_up = Quarters()
    w_dn = Weights("wdn", wdn.at[core], ((0, 208),))
    w_mg = Weights("wmg", wmg, ((0, 4),))

    g_tok.start(0)
    g_tok.start(1)
    across(0, 0, 0)
    across(0, 0, 1)
    for i in (1, 2, 3):
        local[i].wait()
    w_qkv.ahead()
    for i in range(4, 9):
        local[i].wait()

    for j in range(SLOTS):
        gsa[j] = gain_ref[0:1, j * HD : (j + 1) * HD]

    for s in (1, 2, 3, 4):
        for p in (0, 1):
            g_tok.piece(s, p)
            across(s, -s * d_a, p)
            if s < 4:
                across(4 + s, s * d_a, p)
        w_qkv.step(s)
        if s == 2:
            local[9].wait()
            w_up.start()

    def norm(src, gains, out, start, count, rows):

        def chunk(r, carry):
            at = pl.ds(pl.multiple_of(start + r * rows, 16), rows)
            total = src[0, at, :].astype(F32)
            for j in range(1, SLOTS):
                total += src[j, at, :].astype(F32)
            mean = jnp.sum(total, axis=-1, keepdims=True) * (1.0 / D)
            square = jnp.zeros((rows, HD), F32)
            for j in range(SLOTS):
                gap = src[j, at, :].astype(F32) - mean
                square += gap * gap
            var = jnp.sum(square, axis=-1, keepdims=True) * (1.0 / D)
            rstd = lax.rsqrt(var + EPS)
            for j in range(SLOTS):
                gap = src[j, at, :].astype(F32) - mean
                out[j // 2, at, (j % 2) * HD : (j % 2 + 1) * HD] = (gap * rstd * gains[j]).astype(BF16)
            return carry

        lax.fori_loop(0, count // rows, chunk, 0)

    w_up.step(1)

    def token_slot(slot, p):
        return tok.at[slot, pl.ds(p * HALF, HALF)]

    for p in (0, 1):
        arrive("tok_s", p, token_slot(sib, p))
        for s in (1, 2, 3, 4):
            arrive("tok_s", 2 * s + p, token_slot(lax.rem(sib + 2 * s * d_a + 32, 16), p))
            if s < 4:
                arrive("tok_s", 2 * (4 + s) + p, token_slot(lax.rem(sib - 2 * s * d_a + 32, 16), p))
        norm(tok, gsa, xn, p * HALF, HALF, PIECE)
    w_qkv.finish()

    rows2 = TOK // 2

    def project(m):
        def chunk(r, carry):
            at = pl.ds(pl.multiple_of(r * rows2, rows2), rows2)
            total = jnp.zeros((rows2, HD), F32)
            for j in range(NZ):
                total += jnp.dot(xn[j, at, :], wqkv[j, m], preferred_element_type=F32)
            if m == 0:
                qs[at, :] = total.astype(BF16)
            else:
                kv[gx, m - 1, at, :] = total.astype(BF16)
            return carry

        lax.fori_loop(0, 2, chunk, 0, unroll=True)

    def kv_ahead(s, p):
        ref = kv.at[gx_at(-(s - 1) * d_a), p]
        push("kv", 2 * (s - 1) + p, ref, ref, {"gx": gx_at(d_a)})

    def kv_back(s, p):
        ref = kv.at[gx_at((s - 1) * d_a), p]
        push("kv", 8 + 2 * (s - 1) + p, ref, ref, {"gx": gx_at(-d_a)})

    for p in (0, 1):
        project(p + 1)
        kv_ahead(1, p)
        kv_back(1, p)
    project(0)
    for j in range(NY):
        wout_s[j] = wo_ref[:, j * 2 * HD : (j + 1) * 2 * HD]
    for d in range(1, 8):
        to = y_at(d)
        push("wo", d - 1, wout_s.at[to], wout.at[core, ypos], {"gy": gy_at(2 * d)})
    wout[core, ypos] = wout_s[ypos]

    rows4 = TOK // 4

    def attend(block, first=False, part=None):
        start = 0 if part is None else part * HALF
        key_seg = seg8[pl.ds(block, 1), :].astype(F32)

        def chunk(r, carry):
            at = pl.ds(pl.multiple_of(start + r * rows4, 16), rows4)
            scores = lax.dot_general(
                qs[at, :], kv[block, 0], (((1,), (1,)), ((), ())), preferred_element_type=F32
            )
            scores = jnp.where(qseg[at, :] == key_seg, scores, NEG)
            top = jnp.max(scores, axis=-1, keepdims=True)
            if not first:
                old_top = m_s[at, :]
                top = jnp.maximum(old_top, top)
            weights = jnp.exp2((scores - top) * EXP2)
            total = jnp.sum(weights, axis=-1, keepdims=True)
            mixed = jnp.dot(weights.astype(BF16), kv[block, 1], preferred_element_type=F32)
            if not first:
                fade = jnp.exp2((old_top - top) * EXP2)
                total += l_s[at, :] * fade
                mixed += acc_s[at, :] * fade
            m_s[at, :] = top
            l_s[at, :] = total
            acc_s[at, :] = mixed
            return carry

        lax.fori_loop(0, (TOK if part is None else HALF) // rows4, chunk, 0, unroll=True)

    for j in range(NZ):
        seg8[j : j + 1, :] = seg_ref[:, j * TOK : (j + 1) * TOK]
    own_row = seg8[pl.ds(gx, 1), :]
    eye = lax.broadcasted_iota(jnp.int32, (TOK, TOK), 0) == lax.broadcasted_iota(
        jnp.int32, (TOK, TOK), 1
    )
    qseg[...] = jnp.sum(jnp.where(eye, own_row.astype(F32), 0.0), axis=1, keepdims=True)
    for j in range(SLOTS):
        gsm[j] = gain_ref[1:2, j * HD : (j + 1) * HD]
    attend(gx, True)
    w_up.step(2)
    for s in (1, 2, 3, 4):
        for p in (0, 1):
            arrive("kv", 2 * (s - 1) + p, kv.at[gx_at(-s * d_a), p])
            if s < 4:
                kv_ahead(s + 1, p)
                arrive("kv", 8 + 2 * (s - 1) + p, kv.at[gx_at(s * d_a), p])
                if s < 3:
                    kv_back(s + 1, p)
            if s > 1:
                attend(gx_at((-1 if p == 0 else 1) * (s - 1) * d_a))
        if s < 3:
            w_up.step(s + 2)
        if s == 4:
            local[10].wait()
            w_dn.ahead()

    theirs, mine = pl.multiple_of((1 - core) * HALF, HALF), pl.multiple_of(core * HALF, HALF)

    def attended(start):
        at = pl.ds(start, HALF)
        return (acc_s[at, :] / l_s[at, :]).astype(BF16)

    last = gx_at(-4 * d_a)
    attend(last, part=1 - core)
    swap_s[0] = attended(theirs)
    push("swap", 0, swap_s.at[0], att.at[gy], {"gy": sib})
    attend(last, part=core)
    att[gy] = attended(mine)
    g_att.start(0)
    for d in range(1, 8):
        arrive("wo", d - 1, wout.at[core, y_at(-d)])
    push("wo", 7, wout.at[core], wout.at[core], {"gy": sib})
    arrive("swap", 0, att.at[sib])
    g_att.start(1)
    w_dn.step(1)
    for s in (1, 2, 3, 4):
        g_att.step(s)
        if s == 2:
            w_dn.step(2)
        if s == 3:
            local[11].wait()
            w_mg.ahead()
    arrive("wo", 7, wout.at[1 - core])
    w_up.finish()
    push("bulk", 0, wup.at[core], wup.at[core], {"gy": sib})

    for p in (0, 1):
        at = pl.ds(p * PIECE, PIECE)
        total = jnp.zeros((PIECE, 2 * HD), F32)
        for j in range(SLOTS):
            total += jnp.dot(att[j, at, :], wout[j % 2, j // 2], preferred_element_type=F32)
        for h in (0, 1):
            own = tok[2 * ypos + h, pl.ds(pl.multiple_of(mine + p * PIECE, 16), PIECE), :].astype(F32)
            aft[2 * ypos + h, at, :] = (own + total[:, h * HD : (h + 1) * HD]).astype(BF16)
        g_aft.start(p)
    w_dn.step(3)
    for s in (1, 2, 3):
        g_aft.step(s)
        if s == 1:
            w_mg.step(1)
        if s == 2:
            w_dn.step(4)
        if s == 3:
            w_mg.step(2)
            w_dn.finish()
            push("bulk", 1, wdn.at[core], wdn.at[core], {"gy": sib})
    arrive("bulk", 0, wup.at[1 - core])

    def mlp_up(p):
        at = pl.ds(p * PIECE, PIECE)

        def units(g, carry):
            total = jnp.zeros((PIECE, FF_DEV), F32)
            for j in range(NZ):
                total += jnp.dot(xn[j, at, :], wup[g, j], preferred_element_type=F32)
            hid[g, at, :] = erf_gelu(total).astype(BF16)
            return carry

        lax.fori_loop(0, 2, units, 0)

    def mlp_down(d, p):
        dest = y_at(d * d_a)
        part = jnp.zeros((PIECE, 2 * HD), F32)
        for g in (0, 1):
            part += lax.dot_general(
                hid[g, pl.ds(p * PIECE, PIECE), :],
                wdn[g, dest],
                (((1,), (1,)), ((), ())),
                preferred_element_type=F32,
            )
        pp[dest, p, 0] = part[:, :HD].astype(BF16)
        pp[dest, p, 1] = part[:, HD:].astype(BF16)

    def fold(dest, p, extra):
        pp[dest, p] = (pp[dest, p].astype(F32) + extra.astype(F32)).astype(BF16)

    ahead, behind = {"gy": gy_at(2 * d_a)}, {"gy": gy_at(-2 * d_a)}
    far, near = y_at(4 * d_a), y_at(-3 * d_a)
    for p in (0, 1):
        g_aft.piece(4, p)
        norm(aft, gsm, xn, p * PIECE, PIECE, PIECE)
        mlp_up(p)
        if p == 0:
            arrive("bulk", 1, wdn.at[1 - core])
        mlp_down(4, p)
        push("rs_y", p, pp.at[far, p], ra.at[0, p], ahead)
        mlp_down(-3, p)
        push("rs_y", 8 + p, pp.at[near, p], rb.at[0, p], behind)
    w_mg.step(3)
    for d in (3, -2, 2, -1, 1, 0):
        for p in (0, 1):
            mlp_down(d, p)
    for s in (1, 2, 3):
        to_a, to_b = y_at((4 - s) * d_a), y_at(-(3 - s) * d_a)
        for p in (0, 1):
            arrive("rs_y", 2 * (s - 1) + p, ra.at[s - 1, p])
            fold(to_a, p, ra[s - 1, p])
            push("rs_y", 2 * s + p, pp.at[to_a, p], ra.at[s, p], ahead)
        for p in (0, 1):
            if s < 3:
                arrive("rs_y", 8 + 2 * (s - 1) + p, rb.at[s - 1, p])
                fold(to_b, p, rb[s - 1, p])
                push("rs_y", 8 + 2 * s + p, pp.at[to_b, p], rb.at[s, p], behind)
        if s == 1:
            w_mg.step(4)

    def layer_rows(p, h):
        mlp_sum = pp[ypos, p, h].astype(F32) + ra[3, p, h].astype(F32) + rb[2, p, h].astype(F32)
        return (aft[2 * ypos + h, pl.ds(p * PIECE, PIECE), :].astype(F32) + mlp_sum).astype(BF16)

    def rows_at(start, p):
        return pl.ds(pl.multiple_of(start + p * PIECE, 16), PIECE)

    for p in (0, 1):
        arrive("rs_y", 12 + p, rb.at[2, p])
        arrive("rs_y", 6 + p, ra.at[3, p])
        swap_s[1, pl.ds(p * PIECE, PIECE), :] = layer_rows(p, 1 - core)
        push("swap", 1 + p, swap_s.at[1, pl.ds(p * PIECE, PIECE)], lo_s.at[rows_at(mine, p)], {"gy": sib})
        lo_s[rows_at(mine, p), :] = layer_rows(p, core)
    w_mg.finish()
    for p in (0, 1):
        arrive("swap", 1 + p, lo_s.at[rows_at(theirs, p)])

    spot = lax.broadcasted_iota(jnp.int32, (GROUPS, TOK), 1).astype(F32)
    eye2 = lax.broadcasted_iota(jnp.int32, (GROUPS, GROUPS), 0) == lax.broadcasted_iota(
        jnp.int32, (GROUPS, GROUPS), 1
    )
    for k in range(4):
        member = jnp.sum(
            jnp.where(eye2, mg_ref[k : k + 1, :].astype(F32), 0.0), axis=1, keepdims=True
        )
        pick = jnp.where(member == spot, 1.0, 0.0).astype(BF16)
        pk[k] = jnp.dot(pick, lo_s[...], preferred_element_type=F32).astype(BF16)

    others = (4, 3, 5, 2, 6, 1, 7, 0)
    for i, d in enumerate(others):
        dest = y_at(d)
        total = jnp.zeros((GROUPS, 2 * HD), F32)
        for k in range(4):
            total += jnp.dot(pk[k], wmg[dest, k], preferred_element_type=F32)
        mm[0, dest] = total[:, :HD].astype(BF16)
        mm[1, dest] = total[:, HD:].astype(BF16)
        push("mg_s", i, mm.at[1 - core, dest], sm.at[dest], {"gy": sib})
    for i, d in enumerate(others):
        dest = y_at(d)
        arrive("mg_s", i, sm.at[dest])
        mm[core, dest] = (mm[core, dest].astype(F32) + sm[dest].astype(F32)).astype(BF16)
        if d:
            push("mg_y", d - 1, mm.at[core, dest], rm.at[d - 1], {"gy": gy_at(2 * d)})
    lo_ref[...] = jnp.transpose(lo_s[...])
    total = mm[core, ypos].astype(F32)
    for d in range(1, 8):
        arrive("mg_y", d - 1, rm.at[d - 1])
    for d in range(1, 8):
        total += rm[d - 1].astype(F32)
    stk[row] = total.astype(BF16)
    for d in (1, 2, 3):
        push("row", d - 1, stk.at[row], stk.at[row], {"row": row_at(d)})
    wanted = jnp.sum(jnp.where(eye2, src_ref[...].astype(F32), 0.0), axis=1, keepdims=True)
    for d in (1, 2, 3):
        arrive("row", d - 1, stk.at[row_at(-d)])
    place = lax.broadcasted_iota(jnp.int32, (GROUPS, GROUPS), 1).astype(F32)
    total = jnp.zeros((GROUPS, HD), F32)
    for r in range(4):
        pick = jnp.where(wanted == place + float(GROUPS * r), 1.0, 0.0).astype(BF16)
        total += jnp.dot(pick, stk[r], preferred_element_type=F32)
    ret_ref[...] = jnp.transpose(total.astype(BF16))

    for copy in pending:
        copy.wait_send()


def body(
    tokens,
    segments,
    gain_attn,
    w_query,
    w_key,
    w_value,
    w_out,
    gain_mlp,
    w_up,
    w_down,
    w_merge,
    merge_groups,
    sources,
):
    anyspace = pl.BlockSpec(memory_space=pl.ANY)
    vmem = pl.BlockSpec(memory_space=pltpu.VMEM)
    scratch = [
        pltpu.VMEM((SLOTS, TOK, HD), BF16),
        pltpu.VMEM((NZ, TOK, 2 * HD), BF16),
        pltpu.VMEM((NZ, 3, 2 * HD, HD), BF16),
        pltpu.VMEM((TOK, HD), BF16),
        pltpu.VMEM((NZ, 2, TOK, HD), BF16),
        pltpu.VMEM((SLOTS, HALF, HD), BF16),
        pltpu.VMEM((SLOTS, HALF, HD), BF16),
        pltpu.VMEM((NY, HD, 2 * HD), BF16),
        pltpu.VMEM((2, NY, HD, 2 * HD), BF16),
        pltpu.VMEM((2, NZ, 2 * HD, FF_DEV), BF16),
        pltpu.VMEM((2, NZ, 2 * HD, FF_DEV), BF16),
        pltpu.VMEM((NZ, 4, HD, 2 * HD), BF16),
        pltpu.VMEM((2, HALF, FF_DEV), BF16),
        pltpu.VMEM((NY, 2, 2, PIECE, HD), BF16),
        pltpu.VMEM((4, 2, 2, PIECE, HD), BF16),
        pltpu.VMEM((3, 2, 2, PIECE, HD), BF16),
        pltpu.VMEM((TOK, HD), BF16),
        pltpu.VMEM((2, HALF, HD), BF16),
        pltpu.VMEM((4, GROUPS, HD), BF16),
        pltpu.VMEM((2, NY, GROUPS, HD), BF16),
        pltpu.VMEM((NY, GROUPS, HD), BF16),
        pltpu.VMEM((7, GROUPS, HD), BF16),
        pltpu.VMEM((4, GROUPS, HD), BF16),
        pltpu.VMEM((NZ, TOK), jnp.int32),
        pltpu.VMEM((TOK, 1), F32),
        pltpu.VMEM((SLOTS, 1, HD), F32),
        pltpu.VMEM((SLOTS, 1, HD), F32),
        pltpu.VMEM((TOK, 1), F32),
        pltpu.VMEM((TOK, 1), F32),
        pltpu.VMEM((TOK, HD), F32),
        pltpu.VMEM((HD, TOK), BF16),
        pltpu.VMEM((HD, D), BF16),
        pltpu.VMEM((1, NZ * TOK), jnp.int32),
        pltpu.VMEM((4, GROUPS), jnp.int32),
        pltpu.VMEM((1, GROUPS), jnp.int32),
        pltpu.VMEM((2, D), F32),
        pltpu.SemaphoreType.DMA((LOCAL,)),
    ]
    for count in SEM_COUNTS.values():
        scratch += [pltpu.SemaphoreType.DMA((count,)), pltpu.SemaphoreType.DMA((count,))]
    layer_out, returned = pl.pallas_call(
        kernel,
        out_shape=(
            jax.ShapeDtypeStruct((HD, TOK), BF16),
            jax.ShapeDtypeStruct((HD, GROUPS), BF16),
        ),
        in_specs=[anyspace] * 12,
        out_specs=(vmem, vmem),
        scratch_shapes=scratch,
        compiler_params=pltpu.CompilerParams(
            collective_id=0, has_side_effects=True, vmem_limit_bytes=60 << 20
        ),
        name="layer",
    )(
        tokens[0].T,
        segments,
        jnp.stack([gain_attn, gain_mlp]),
        w_query,
        w_key,
        w_value,
        w_out,
        w_up,
        w_down.T,
        w_merge,
        merge_groups[0].T,
        sources,
    )
    return (layer_out.T[None], returned.T[None])


def solution(mesh):
    placed = (
        P("row", "gx", "gy"),
        P("row", None),
        P(),
        P("gx", "gy"),
        P("gx", "gy"),
        P("gx", "gy"),
        P("gy", None),
        P(),
        P("gx", "gy"),
        P("gy", "gx"),
        P(None, "gy", "gx"),
        P("row", "gx", None),
        P("row", "gx"),
    )
    return jax.shard_map(
        body,
        mesh=mesh,
        in_specs=placed,
        out_specs=(P("row", "gx", "gy"), P("row", "gx", "gy")),
        check_vma=False,
    )
```
